256 devices in a mesh: plane: 4 (over x), wire: 4 (over z_lo), tick: 16 (over z_hi, y, core).
Axes of the slice: x: 4, y: 4, z: 8 (z_hi: 2, z_lo: 4; z = z_hi * 4 + z_lo), core: 2. Of those that a mesh axis runs over, the one named last changes fastest.
Arguments:
- raw: bfloat16 [4096, 32768], P(('plane', 'wire'), 'tick'), may hold values from -6 to 6
- chan_mask: int32 [4096], P(('plane', 'wire')), may hold values 0 or 1
- kernel: bfloat16 [4, 21, 256], P('plane'), may hold values from -0.078125 to 0.078125
- geometry: bfloat16 [128, 32, 128], replicated, may hold values from -1 to 1
- roi_block: int32 [26112], P(('plane', 'wire', 'tick')), may hold values from 0 to 127, as said below
- roi_owner: int32 [26112], P(('plane', 'wire', 'tick')), may hold values from 0 to 15, as said below
Outputs:
- signal: bfloat16 [4096, 32768], P(('plane', 'wire'), 'tick')
- image: float32 [2048, 32768], P(('plane', 'wire'), 'tick')
The draws below stay inside these ranges and needn't reach their ends.
Inputs may be any that keep to these rules, and one draw needn't show every extreme that they name: `roi_block`: the 102 ids of one device are distinct. `roi_owner`: owner o is the device of the same tick shard whose index over plane and wire together is o. A device names one owner in at most 25 slots; in every tick shard one owner is named in exactly 25 slots by every device of that shard.
All inputs are finite; a program needn't handle non-finite values. No bound on the sum of `chan_mask` on one device may be relied on, other than what follows from the above.
Results may differ from the reference program's by a relative error of at most 0.0029.
Values may be sent and summed in bfloat16 or wider, within the bound.
A program may use at most 64 MiB of HBM per device.

```python
import jax
import jax.numpy as jnp
from jax import lax

WD = 256
TK = 2048
KW = 21
KT = 256
WB = 32
TB = 128
CELLS = 128
WBLK = 8
TBLK = 16
NBLK = 128
SLOTS = 102
CAP = 25
OWNERS = 16
TSHARDS = 16
WIRES = 4096
TICKS = 32768
GEOS = 128
N_PLANE = 4
N_WIRE = 4
N_TICK = 16


def roi_tables(key):
    base = jax.random.fold_in(key, 7)
    hot_key, dev_key = jax.random.split(base, 2)
    hot_owner = jax.random.randint(hot_key, (TSHARDS,), 0, OWNERS)

    def one_device(dev_rng, device):
        perm_key, shift_key, order_key = jax.random.split(dev_rng, 3)
        block_list = jax.random.permutation(perm_key, NBLK)[:SLOTS]
        target = hot_owner[device % TSHARDS]
        positions = jnp.arange(SLOTS, dtype=jnp.int32)
        shift = jax.random.randint(shift_key, (), 0, OWNERS - 1)
        others = (target + 1 + (positions - CAP + shift) % (OWNERS - 1)) % OWNERS
        dest_list = jnp.where(positions < CAP, target, others)
        order = jax.random.permutation(order_key, SLOTS)
        return (block_list, dest_list[order])
    dev_keys = jax.random.split(dev_key, OWNERS * TSHARDS)
    block_all, dest_all = jax.vmap(one_device)(dev_keys, jnp.arange(OWNERS * TSHARDS, dtype=jnp.int32))
    return (block_all.reshape(-1).astype(jnp.int32), dest_all.reshape(-1).astype(jnp.int32))


def draw_roi_block(key, part):
    return roi_tables(key)[0]


def draw_roi_owner(key, part):
    return roi_tables(key)[1]


def plant(array, rng, low, top_value):
    dims = array.shape
    place = [jax.random.randint(jax.random.fold_in(rng, axis), (), 0, dims[axis]) for axis in range(len(dims))]
    array = array.at[tuple(place)].set(low)
    longest = dims.index(max(dims))
    place[longest] = (place[longest] + 1) % dims[longest]
    return array.at[tuple(place)].set(top_value)


def block_levels(rng, extent, cuts, smallest, top_value):
    def one(position, parts):
        steps = jax.random.uniform(jax.random.fold_in(jax.random.fold_in(rng, 6), position), (parts,), jnp.float32, smallest / len(cuts), top_value / len(cuts))
        return jnp.repeat(jnp.exp(steps), extent[position] // parts).reshape((-1,) + (1,) * (len(extent) - position - 1))

    loudness = one(*cuts[0])
    for cut in cuts[1:]:
        loudness = loudness * one(*cut)
    return loudness


def scatter_about(key, extent, width, bound, cuts=(), kind=jnp.bfloat16):
    drawn = width * jax.random.normal(key, extent, jnp.float32)
    if cuts:
        drawn = drawn * block_levels(key, extent, cuts, -0.22, 0.18)
    return jnp.clip(drawn, -bound, bound).astype(kind)


def setup_inputs(seed: int = 0) -> dict:
    key_list = jax.random.split(jax.random.key(seed), 7)
    return {
        "raw": scatter_about(key_list[0], (WIRES, TICKS), 1.0, 6.0, ((0, 16), (1, 16))),
        "chan_mask": plant((jax.random.randint(key_list[1], (WIRES,), 0, 16) < 15).astype(jnp.int32), jax.random.fold_in(key_list[1], 1), 0, 1),
        "kernel": scatter_about(key_list[2], (N_PLANE, KW, KT), (KW * KT) ** -0.5, 0.078125, ((0, 4),)),
        "geometry": scatter_about(key_list[3], (GEOS, WB, CELLS), WB ** -0.5, 1.0),
        "roi_block": draw_roi_block(jax.random.fold_in(key_list[6], 71), 0),
        "roi_owner": draw_roi_owner(jax.random.fold_in(key_list[6], 71), 0),
    }


def reference(raw, chan_mask, kernel, geometry, roi_block, roi_owner):
    group_wires = N_WIRE * WD
    half_w = KW // 2
    half_t = KT // 2
    fft_length = TICKS + KT
    masked = raw * chan_mask[:, None].astype(jnp.bfloat16)
    planes_in = masked.astype(jnp.float32).reshape(N_PLANE, group_wires, TICKS)

    def deconvolve(pieces):
        plane_data, plane_kernel = pieces
        spectrum = jnp.fft.rfft(plane_data, n=fft_length, axis=-1)
        spectrum = jnp.pad(spectrum, ((half_w, half_w), (0, 0)))
        kernel_spec = jnp.fft.rfft(plane_kernel.astype(jnp.float32), n=fft_length, axis=-1)
        accum = jnp.zeros((group_wires, spectrum.shape[1]), spectrum.dtype)
        for tap_index in range(KW):
            accum = accum + kernel_spec[tap_index][None, :] * spectrum[tap_index:tap_index + group_wires]
        return jnp.fft.irfft(accum, n=fft_length, axis=-1)[:, half_t:half_t + TICKS]

    filtered = lax.map(deconvolve, (planes_in, kernel))
    signal = filtered.reshape(WIRES, TICKS).astype(jnp.bfloat16)

    grid = signal.reshape(N_PLANE, N_WIRE, WBLK, WB, N_TICK, TBLK, TB)
    block_tiles = grid.transpose(4, 0, 1, 2, 5, 3, 6).reshape(N_TICK, OWNERS, NBLK, WB, TB)
    block_ids = roi_block.reshape(OWNERS, N_TICK, SLOTS).transpose(1, 0, 2)
    owner_ids = roi_owner.reshape(OWNERS, N_TICK, SLOTS).transpose(1, 0, 2)

    def per_tick(pieces):
        tiles_now, ids_now, owners_now = pieces
        chosen = jnp.take_along_axis(tiles_now, ids_now[:, :, None, None], axis=1)
        chosen = chosen.reshape(OWNERS * SLOTS, WB, TB).astype(jnp.float32)
        geo_index = (jnp.arange(OWNERS, dtype=jnp.int32)[:, None] * WBLK + ids_now // TBLK).reshape(-1)
        geo_rows = geometry[geo_index].astype(jnp.float32)
        products = jnp.einsum('swc,swt->sct', geo_rows, chosen, precision=lax.Precision.HIGHEST)
        seg_keys = (owners_now * TBLK + ids_now % TBLK).reshape(-1).astype(jnp.int32)
        summed = jax.ops.segment_sum(products, seg_keys, num_segments=OWNERS * TBLK)
        return summed.reshape(OWNERS, TBLK, CELLS, TB).transpose(0, 2, 1, 3).reshape(OWNERS, CELLS, TK)

    images = lax.map(per_tick, (block_tiles, block_ids, owner_ids))
    image = images.transpose(1, 2, 0, 3).reshape(OWNERS * CELLS, TICKS)
    return signal, image
```

```python
import jax
import jax.numpy as jnp
from jax import lax
from jax.experimental import pallas as pl
from jax.experimental.pallas import tpu as pltpu
from jax.sharding import PartitionSpec as P

TB = 128
VMEM = pl.BlockSpec(memory_space=pltpu.VMEM)
LIMIT = 48 << 20


def with_halo(array, sides, width):
    for axis, dim in sides:
        devices, length = (lax.axis_size(axis), array.shape[dim])
        up = [(i, (i + 1) % devices) for i in range(devices - 1)]
        down = [(j, i) for i, j in up]
        last = lax.slice_in_dim(array, length - width, length, axis=dim)
        leading = lax.slice_in_dim(array, 0, width, axis=dim)
        before = lax.ppermute(last, axis, up)
        after = lax.ppermute(leading, axis, down)
        array = jnp.concatenate([before, array, after], axis=dim)
    return array


def bands_kernel(taps_ref, out_ref):
    row = lax.broadcasted_iota(jnp.int32, (TB, TB), 0)
    col = lax.broadcasted_iota(jnp.int32, (TB, TB), 1)
    upper = col >= row
    zero = jnp.zeros((TB, TB), jnp.float32)
    for a in range(22):
        m, p = a // 2, a % 2
        rolled = [
            pltpu.roll(
                jnp.broadcast_to(taps_ref[a : a + 1, half * TB : (half + 1) * TB], (TB, TB)),
                0,
                1,
                stride=1,
                stride_axis=0,
            )
            for half in range(2)
        ]
        pieces = (
            jnp.where(upper, zero, rolled[1]),
            jnp.where(upper, rolled[1], rolled[0]),
            jnp.where(upper, rolled[0], zero),
        )
        for piece in range(3):
            start = (m * 3 + piece) * TB
            out_ref[start : start + TB, p * TB : (p + 1) * TB] = pieces[piece].astype(jnp.bfloat16)


def make_bands(taps):
    padded = jnp.zeros((24, 2 * TB), jnp.float32).at[: taps.shape[0]].set(taps.astype(jnp.float32))
    return pl.pallas_call(
        bands_kernel,
        out_shape=jax.ShapeDtypeStruct((33 * TB, 2 * TB), jnp.bfloat16),
        in_specs=[VMEM],
        out_specs=VMEM,
        name="bands",
    )(padded)


CHUNK = 64


def deconv_kernel(wave_ref, band_ref, out_ref, tall_ref, shift_ref, sum_ref):
    def spread(i, carry):
        for j in range(18):
            piece = wave_ref[pl.ds(pl.multiple_of(i * 16, 16), 16), j * TB : (j + 1) * TB]
            tall_ref[pl.ds(i * 288 + j, 16, stride=18), :] = piece.astype(jnp.float32)
        return carry

    lax.fori_loop(0, 18, spread, 0)

    def window(i, carry):
        for u in range(8):
            wire = i * 8 + u
            for piece in range(3):
                shift_ref[piece, wire] = tall_ref[pl.ds(wire * 18 + piece, 16), :].astype(jnp.bfloat16)
        return carry

    lax.fori_loop(0, 35, window, 0)

    rows = CHUNK * 16

    def chunk(c, carry):
        first = c * CHUNK
        lhs = jnp.concatenate(
            [
                shift_ref[piece, pl.ds(first + 2 * m, CHUNK + 1)].reshape((CHUNK + 1) * 16, TB)
                for m in range(11)
                for piece in range(3)
            ],
            axis=1,
        )
        both = jnp.dot(lhs, band_ref[...], preferred_element_type=jnp.float32)
        sum_ref[...] = both[:rows, :TB] + both[16:, TB:]
        for j in range(16):
            for b in range(CHUNK // 16):
                start = pl.multiple_of(first + b * 16, 16)
                out_ref[j, pl.ds(start, 16), :] = sum_ref[pl.ds(b * 256 + j, 16, stride=16), :].astype(
                    jnp.bfloat16
                )
        return carry

    lax.fori_loop(0, 256 // CHUNK, chunk, 0)


def deconvolve(padded, bands):
    return pl.pallas_call(
        deconv_kernel,
        out_shape=jax.ShapeDtypeStruct((16, 256, TB), jnp.bfloat16),
        in_specs=[VMEM, VMEM],
        out_specs=VMEM,
        scratch_shapes=[
            pltpu.VMEM((288 * 18, TB), jnp.float32),
            pltpu.VMEM((3, 280, 16, TB), jnp.bfloat16),
            pltpu.VMEM((CHUNK * 16, TB), jnp.float32),
        ],
        compiler_params=pltpu.CompilerParams(vmem_limit_bytes=LIMIT),
        name="deconvolve",
    )(padded, bands)


GROUP = 4


def image_kernel(tiles_ref, geo_ref, owner_ref, out_ref, lhs_ref, total_ref):
    for g in range(16 // GROUP):
        for s in range(GROUP):
            source = g * GROUP + s
            cols = slice(source * 256, (source + 1) * 256)
            owners = owner_ref[source : source + 1, :]
            geo = geo_ref[:, cols]
            for o in range(16):
                keep = jnp.where(owners == o, jnp.float32(1), jnp.float32(0)).astype(jnp.bfloat16)
                lhs_ref[o * TB : (o + 1) * TB, s * 256 : (s + 1) * 256] = geo * keep
        tiles = tiles_ref[g * GROUP : (g + 1) * GROUP].reshape(GROUP * 256, TB)
        part = jnp.dot(lhs_ref[...], tiles, preferred_element_type=jnp.float32)
        if g == 0:
            total_ref[...] = part
        elif g < 16 // GROUP - 1:
            total_ref[...] += part
        else:
            out_ref[...] = (total_ref[...] + part).astype(jnp.bfloat16)


def make_image(tiles, geo, owners):
    return pl.pallas_call(
        image_kernel,
        out_shape=jax.ShapeDtypeStruct((16 * TB, TB), jnp.bfloat16),
        in_specs=[VMEM] * 3,
        out_specs=VMEM,
        scratch_shapes=[
            pltpu.VMEM((16 * TB, GROUP * 256), jnp.bfloat16),
            pltpu.VMEM((16 * TB, TB), jnp.float32),
        ],
        compiler_params=pltpu.CompilerParams(vmem_limit_bytes=LIMIT),
        name="image",
    )(tiles, geo, owners)


def shards(raw, chan_mask, kernel, geometry, roi_block, roi_owner):
    masked = raw * chan_mask[:, None].astype(jnp.bfloat16)
    padded = with_halo(masked, (("tick", 1),), TB)
    padded = with_halo(padded, (("wire", 0),), 10)
    padded = jnp.pad(padded, ((0, 12), (0, 0)))
    tiles = deconvolve(padded, make_bands(kernel[0]))
    signal = tiles.transpose(1, 0, 2).reshape(256, 2048)

    hit = roi_block[:, None] == jnp.arange(128, dtype=jnp.int32)[None, :]
    owner = jnp.sum(jnp.where(hit, roi_owner[:, None] + 1, 0), axis=0) - 1
    owner = jnp.repeat(owner.reshape(8, 16).T, 32, axis=1).astype(jnp.bfloat16)
    group = ("plane", "wire")
    owners = lax.all_to_all(owner, group, split_axis=0, concat_axis=0, tiled=True)
    geo = geometry.reshape(4096, 128).T
    arrived = lax.all_to_all(tiles, group, split_axis=0, concat_axis=0, tiled=True)
    pieces = make_image(arrived, geo, owners.astype(jnp.int32))
    pieces = lax.all_to_all(pieces.reshape(16, TB, TB), group, split_axis=0, concat_axis=0, tiled=True)
    image = pieces.transpose(1, 0, 2).reshape(TB, 2048).astype(jnp.float32)
    return (signal, image)


def solution(mesh):
    in_specs = (
        P(("plane", "wire"), "tick"),
        P(("plane", "wire")),
        P("plane", None, None),
        P(),
        P(("plane", "wire", "tick")),
        P(("plane", "wire", "tick")),
    )
    out_specs = (P(("plane", "wire"), "tick"), P(("plane", "wire"), "tick"))
    return jax.shard_map(shards, mesh=mesh, in_specs=in_specs, out_specs=out_specs, check_vma=False)
```

```python
import jax
import jax.numpy as jnp
from jax import lax
from jax.experimental import pallas as pl
from jax.experimental.pallas import tpu as pltpu
from jax.sharding import PartitionSpec as P

TB = 128
N = 16
CHUNK = 64
ROWS = CHUNK * 16
MESH = pl.DeviceIdType.MESH
VMEM = pl.BlockSpec(memory_space=pltpu.VMEM)
ANY = pl.BlockSpec(memory_space=pl.ANY)
BF16 = jnp.bfloat16
F32 = jnp.float32


def row_of(ref, index, size):
    return ref.at[pl.ds(pl.multiple_of(index, size), size)]


def build_bands(taps_ref, band_ref):
    row = lax.broadcasted_iota(jnp.int32, (TB, TB), 0)
    col = lax.broadcasted_iota(jnp.int32, (TB, TB), 1)
    upper = col >= row
    zero = jnp.zeros((TB, TB), F32)

    def pair(m, carry):
        for p in range(2):
            taps = taps_ref[pl.ds(2 * m + p, 1), :]
            low, high = [
                pltpu.roll(
                    jnp.broadcast_to(taps[:, half * TB : (half + 1) * TB], (TB, TB)),
                    0,
                    1,
                    stride=1,
                    stride_axis=0,
                )
                for half in range(2)
            ]
            pieces = (
                jnp.where(upper, zero, high),
                jnp.where(upper, high, low),
                jnp.where(upper, low, zero),
            )
            for piece in range(3):
                start = pl.multiple_of((m * 3 + piece) * TB, TB)
                band_ref[pl.ds(start, TB), p * TB : (p + 1) * TB] = pieces[piece].astype(BF16)
        return carry

    lax.fori_loop(0, 11, pair, 0)


def kernel(
    raw_ref,
    mask_ref,
    taps_ref,
    roi_ref,
    geo_ref,
    signal_ref,
    image_ref,
    edge_t,
    edge_w,
    halo_t,
    halo_w,
    halo_c,
    mask_col,
    tall,
    shifted,
    band,
    sums,
    sig,
    recv,
    own_out,
    own_in,
    geo,
    geo_t,
    masked_geo,
    total,
    piece_out,
    piece_in,
    halo_send,
    halo_recv,
    own_send,
    own_recv,
    tile_send,
    tile_recv,
    image_send,
    image_recv,
    local,
):
    plane, wire, tick = lax.axis_index("plane"), lax.axis_index("wire"), lax.axis_index("tick")
    me = plane * 4 + wire
    up_t, down_t = lax.rem(tick + 1, 16), lax.rem(tick + 15, 16)
    up_w, down_w = lax.rem(wire + 1, 4), lax.rem(wire + 3, 4)

    def member(m):
        return (m // 4, lax.rem(m, 4), tick)

    barrier = pltpu.get_barrier_semaphore()

    def greet(r, carry):
        pl.semaphore_signal(barrier, inc=1, device_id=member(lax.rem(me + r, N)), device_id_type=MESH)
        return carry

    for w in (wire, up_w, down_w):
        for t in (up_t, down_t):
            pl.semaphore_signal(barrier, inc=1, device_id=(plane, w, t), device_id_type=MESH)
    lax.fori_loop(1, N, greet, 0)

    geo_copy = pltpu.make_async_copy(geo_ref, geo, local.at[0])
    geo_copy.start()

    row = lax.broadcasted_iota(jnp.int32, (256, 256), 0)
    col = lax.broadcasted_iota(jnp.int32, (256, 256), 1)
    diag = jnp.where(row == col, mask_ref[...].astype(F32), 0.0).astype(BF16)
    mask_col[...] = jnp.dot(diag, jnp.ones((256, TB), BF16), preferred_element_type=F32)

    ids = roi_ref[0:1, :]
    owner = roi_ref[1:2, :]
    tick_hit = jnp.where(
        lax.broadcasted_iota(jnp.int32, (N, TB), 0) == lax.rem(ids, 16), 1.0, 0.0
    ).astype(BF16)
    wire_hit = jnp.where(
        lax.broadcasted_iota(jnp.int32, (256, TB), 0) // 32 == ids // 16, (owner + 1).astype(F32), 0.0
    ).astype(BF16)
    table = lax.dot_general(tick_hit, wire_hit, (((1,), (1,)), ((), ())), preferred_element_type=F32)
    for m in range(N):
        for half in range(2):
            own_out[m, half : half + 1, :] = table[m : m + 1, half * TB : (half + 1) * TB]
        own_out[m, 2:8, :] = jnp.zeros((6, TB), F32)

    for side, start in ((0, 0), (1, 15 * TB)):
        edge_t[side] = (raw_ref[:, start : start + TB].astype(F32) * mask_col[...]).astype(BF16)
    for side, start in ((0, 0), (1, 240)):
        for j in range(N):
            cols = slice(j * TB, (j + 1) * TB)
            edge_w[side, :, cols] = (
                raw_ref[start : start + 16, cols].astype(F32) * mask_col[start : start + 16, :]
            ).astype(BF16)

    pl.semaphore_wait(barrier, 21)

    first, last = slice(0, TB), slice(15 * TB, 16 * TB)
    halo_copies = [
        pltpu.make_async_remote_copy(
            src_ref=src,
            dst_ref=dst,
            send_sem=halo_send.at[i],
            recv_sem=halo_recv.at[i],
            device_id=(plane, w, t),
            device_id_type=MESH,
        )
        for i, (src, dst, w, t) in enumerate(
            (
                (edge_t.at[1], halo_t.at[0], wire, up_t),
                (edge_t.at[0], halo_t.at[1], wire, down_t),
                (edge_w.at[1], halo_w.at[0], up_w, tick),
                (edge_w.at[0], halo_w.at[1], down_w, tick),
                (edge_w.at[1, :, last], halo_c.at[0], up_w, up_t),
                (edge_w.at[1, :, first], halo_c.at[1], up_w, down_t),
                (edge_w.at[0, :, last], halo_c.at[2], down_w, up_t),
                (edge_w.at[0, :, first], halo_c.at[3], down_w, down_t),
            )
        )
    ]
    for copy in halo_copies:
        copy.start()

    def own_copy(m, source):
        return pltpu.make_async_remote_copy(
            src_ref=own_out.at[m],
            dst_ref=own_in.at[source],
            send_sem=own_send.at[m],
            recv_sem=own_recv.at[source],
            device_id=member(m),
            device_id_type=MESH,
        )

    def send_own(r, carry):
        own_copy(lax.rem(me + r, N), me).start()
        return carry

    lax.fori_loop(1, N, send_own, 0)
    own_in[me] = own_out[me]

    build_bands(taps_ref, band)

    def spread(i, carry):
        wires = pl.ds(pl.multiple_of(i * 16, 16), 16)
        keep = mask_col[wires, :]
        for j in range(N):
            piece = raw_ref[wires, j * TB : (j + 1) * TB].astype(F32) * keep
            tall[pl.ds((i + 1) * 288 + j + 1, 16, stride=18), :] = piece
        return carry

    lax.fori_loop(0, 16, spread, 0)

    tick_ok = [jnp.where(tick == 0, 0.0, 1.0), jnp.where(tick == 15, 0.0, 1.0)]
    wire_ok = [jnp.where(wire == 0, 0.0, 1.0), jnp.where(wire == 3, 0.0, 1.0)]

    def window(i, carry):
        for u in range(8):
            slot = i * 8 + u
            for piece in range(3):
                shifted[piece, slot] = tall[pl.ds(slot * 18 + piece, 16), :].astype(BF16)
        return carry

    for side in range(2):
        halo_copies[side].wait_recv()

    def spread_ticks(i, carry):
        wires = pl.ds(pl.multiple_of(i * 16, 16), 16)
        for side, j in ((0, 0), (1, 17)):
            tall[pl.ds((i + 1) * 288 + j, 16, stride=18), :] = (
                halo_t[side, wires, :].astype(F32) * tick_ok[side]
            )
        return carry

    lax.fori_loop(0, 16, spread_ticks, 0)
    lax.fori_loop(2, 34, window, 0)

    def tile_copy(m, source, part):
        return pltpu.make_async_remote_copy(
            src_ref=sig.at[m, part],
            dst_ref=recv.at[source, part],
            send_sem=tile_send.at[m],
            recv_sem=tile_recv.at[source],
            device_id=member(m),
            device_id_type=MESH,
        )

    def run_chunk(c):
        base = c * CHUNK
        lhs = jnp.concatenate(
            [
                shifted[piece, pl.ds(base + 6 + 2 * m, CHUNK + 1)].reshape((CHUNK + 1) * 16, TB)
                for m in range(11)
                for piece in range(3)
            ],
            axis=1,
        )
        both = jnp.dot(lhs, band[...], preferred_element_type=F32)
        sums[...] = both[:ROWS, :TB] + both[16:, TB:]
        for j in range(N):
            for b in range(CHUNK // 16):
                start = pl.multiple_of(base + b * 16, 16)
                sig[j, pl.ds(start, 16), :] = sums[pl.ds(b * 256 + j, 16, stride=16), :].astype(BF16)
        part = pl.ds(pl.multiple_of(base, CHUNK), CHUNK)

        def send(r, carry):
            tile_copy(lax.rem(me + r, N), me, part).start()
            return carry

        lax.fori_loop(1, N, send, 0)

    def middle(i, carry):
        run_chunk(i + 1)
        return carry

    lax.fori_loop(0, 2, middle, 0)

    for copy in halo_copies[2:]:
        copy.wait_recv()
    for side, base in ((0, 0), (1, 272 * 18)):
        for j in range(N):
            tall[pl.ds(base + j + 1, 16, stride=18), :] = (
                halo_w[side, :, j * TB : (j + 1) * TB].astype(F32) * wire_ok[side]
            )
        for t, j in ((0, 0), (1, 17)):
            tall[pl.ds(base + j, 16, stride=18), :] = (
                halo_c[side * 2 + t].astype(F32) * wire_ok[side] * tick_ok[t]
            )
    lax.fori_loop(0, 2, window, 0)
    lax.fori_loop(34, 36, window, 0)

    def outer(i, carry):
        run_chunk(i * 3)
        return carry

    lax.fori_loop(0, 2, outer, 0)

    def store_signal(j, carry):
        pltpu.make_async_copy(
            sig.at[j], signal_ref.at[:, pl.ds(pl.multiple_of(j * TB, TB), TB)], local.at[1]
        ).start()
        return carry

    lax.fori_loop(0, N, store_signal, 0)
    keep_tile = pltpu.make_async_copy(sig.at[me], recv.at[me], local.at[2])
    keep_tile.start()

    geo_copy.wait()
    row = lax.broadcasted_iota(jnp.int32, (TB, TB), 0)
    col = lax.broadcasted_iota(jnp.int32, (TB, TB), 1)
    eye = jnp.where(row == col, 1.0, 0.0).astype(BF16)

    def turn(s, carry):
        rows = pl.ds(pl.multiple_of(s * 256, 256), 256)
        geo_t[s] = lax.dot_general(
            eye, geo[rows, :], (((1,), (1,)), ((), ())), preferred_element_type=F32
        ).astype(BF16)
        return carry

    lax.fori_loop(0, N, turn, 0)

    def wait_own(r, carry):
        other = lax.rem(me + r, N)
        own_copy(other, other).wait()
        return carry

    lax.fori_loop(1, N, wait_own, 0)

    def source_of(g, i):
        return lax.rem(plane + i, 4) * 4 + lax.rem(wire + g, 4)

    def mask_geo(g, carry):
        for i in range(4):
            s = source_of(g, i)
            for half in range(2):
                owners = own_in[s, half : half + 1, :]
                part = geo_t[s, :, half * TB : (half + 1) * TB]
                for o in range(N):
                    keep = jnp.where(owners == o + 1, 1.0, 0.0).astype(BF16)
                    start = i * 256 + half * TB
                    masked_geo[g, o, :, start : start + TB] = part * keep
        return carry

    lax.fori_loop(0, 4, mask_geo, 0)
    keep_tile.wait()

    def image_copy(o, source):
        return pltpu.make_async_remote_copy(
            src_ref=piece_out.at[o],
            dst_ref=piece_in.at[source],
            send_sem=image_send.at[o],
            recv_sem=image_recv.at[source],
            device_id=member(o),
            device_id_type=MESH,
        )

    everything = pl.ds(0, 256)
    for g in range(4):
        for i in range(4):
            if g or i:
                s = source_of(g, i)
                tile_copy(s, s, everything).wait_recv()
        tiles = jnp.concatenate([recv[source_of(g, i)] for i in range(4)], axis=0)
        for k in range(4):
            members = [lax.rem(me + 1 + 4 * k + i, N) for i in range(4)]
            lhs = jnp.concatenate([masked_geo[g, o] for o in members], axis=0)
            part = jnp.dot(lhs, tiles, preferred_element_type=F32)
            for i, o in enumerate(members):
                now = part[i * TB : (i + 1) * TB]
                if g == 0:
                    total[o] = now
                elif g < 3:
                    total[o] += now
                else:
                    piece_out[o] = (total[o] + now).astype(BF16)
                    if k * 4 + i < N - 1:
                        image_copy(o, me).start()
                    else:
                        piece_in[o] = piece_out[o]

    pltpu.make_async_copy(signal_ref, signal_ref, local.at[1]).wait()
    for copy in halo_copies:
        copy.wait_send()

    def wait_tiles(r, carry):
        tile_copy(lax.rem(me + r, N), me, everything).wait_send()
        return carry

    lax.fori_loop(1, N, wait_tiles, 0)

    def wait_image(r, carry):
        other = lax.rem(me + r, N)
        image_copy(other, other).wait()
        return carry

    lax.fori_loop(1, N, wait_image, 0)
    image_ref[...] = piece_in[...]


def fused(raw, mask, taps, roi, geo):
    dma = pltpu.SemaphoreType.DMA
    return pl.pallas_call(
        kernel,
        out_shape=(
            jax.ShapeDtypeStruct((256, 2048), BF16),
            jax.ShapeDtypeStruct((N, TB, TB), BF16),
        ),
        in_specs=[VMEM, VMEM, VMEM, VMEM, ANY],
        out_specs=(ANY, VMEM),
        scratch_shapes=[
            pltpu.VMEM((2, 256, TB), BF16),
            pltpu.VMEM((2, 16, 2048), BF16),
            pltpu.VMEM((2, 256, TB), BF16),
            pltpu.VMEM((2, 16, 2048), BF16),
            pltpu.VMEM((4, 16, TB), BF16),
            pltpu.VMEM((256, TB), F32),
            pltpu.VMEM((288 * 18, TB), F32),
            pltpu.VMEM((3, 288, 16, TB), BF16),
            pltpu.VMEM((33 * TB, 2 * TB), BF16),
            pltpu.VMEM((ROWS, TB), F32),
            pltpu.VMEM((N, 256, TB), BF16),
            pltpu.VMEM((N, 256, TB), BF16),
            pltpu.VMEM((N, 8, TB), F32),
            pltpu.VMEM((N, 8, TB), F32),
            pltpu.VMEM((4096, TB), BF16),
            pltpu.VMEM((N, TB, 256), BF16),
            pltpu.VMEM((4, N, TB, 1024), BF16),
            pltpu.VMEM((N, TB, TB), F32),
            pltpu.VMEM((N, TB, TB), BF16),
            pltpu.VMEM((N, TB, TB), BF16),
            dma((8,)),
            dma((8,)),
            dma((N,)),
            dma((N,)),
            dma((N,)),
            dma((N,)),
            dma((N,)),
            dma((N,)),
            dma((3,)),
        ],
        compiler_params=pltpu.CompilerParams(
            vmem_limit_bytes=56 << 20, collective_id=0, has_side_effects=True
        ),
        name="fused",
    )(raw, mask, taps, roi, geo)


def shards(raw, chan_mask, kernel_rows, geometry, roi_block, roi_owner):
    taps = jnp.zeros((24, 2 * TB), F32).at[:21].set(kernel_rows[0].astype(F32))
    slots = roi_block.shape[0]
    roi = jnp.full((2, TB), -1, jnp.int32).at[:, :slots].set(jnp.stack([roi_block, roi_owner]))
    signal, pieces = fused(raw, chan_mask.reshape(1, 256), taps, roi, geometry.reshape(4096, TB))
    image = pieces.transpose(1, 0, 2).reshape(TB, 2048).astype(F32)
    return (signal, image)


def solution(mesh):
    in_specs = (
        P(("plane", "wire"), "tick"),
        P(("plane", "wire")),
        P("plane", None, None),
        P(),
        P(("plane", "wire", "tick")),
        P(("plane", "wire", "tick")),
    )
    out_specs = (P(("plane", "wire"), "tick"), P(("plane", "wire"), "tick"))
    return jax.shard_map(shards, mesh=mesh, in_specs=in_specs, out_specs=out_specs, check_vma=False)
```

```python
import jax
import jax.numpy as jnp
from jax import lax
from jax.experimental import pallas as pl
from jax.experimental.pallas import tpu as pltpu
from jax.sharding import PartitionSpec as P

TB = 128
N = 16
CHUNK = 64
ROWS = CHUNK * 16
MESH = pl.DeviceIdType.MESH
VMEM = pl.BlockSpec(memory_space=pltpu.VMEM)
ANY = pl.BlockSpec(memory_space=pl.ANY)
BF16 = jnp.bfloat16
F32 = jnp.float32


def row_of(ref, index, size):
    return ref.at[pl.ds(pl.multiple_of(index, size), size)]


def build_bands(taps_ref, band_ref):
    row = lax.broadcasted_iota(jnp.int32, (TB, TB), 0)
    col = lax.broadcasted_iota(jnp.int32, (TB, TB), 1)
    upper = col >= row
    zero = jnp.zeros((TB, TB), F32)

    def pair(m, carry):
        for p in range(2):
            taps = taps_ref[pl.ds(2 * m + p, 1), :]
            low, high = [
                pltpu.roll(
                    jnp.broadcast_to(taps[:, half * TB : (half + 1) * TB], (TB, TB)),
                    0,
                    1,
                    stride=1,
                    stride_axis=0,
                )
                for half in range(2)
            ]
            pieces = (
                jnp.where(upper, zero, high),
                jnp.where(upper, high, low),
                jnp.where(upper, low, zero),
            )
            for piece in range(3):
                start = pl.multiple_of((m * 3 + piece) * TB, TB)
                band_ref[pl.ds(start, TB), p * TB : (p + 1) * TB] = pieces[piece].astype(BF16)
        return carry

    lax.fori_loop(0, 11, pair, 0)


def kernel(
    raw_hbm,
    mask_ref,
    taps_ref,
    block_ref,
    owner_ref,
    geo_ref,
    signal_ref,
    image_ref,
    raw_ref,
    taps,
    roi_ref,
    edge_t,
    edge_w,
    halo_t,
    halo_w,
    halo_c,
    mask_col,
    tall,
    shifted,
    band,
    sums,
    sig,
    recv,
    own_out,
    own_in,
    geo,
    geo_t,
    masked_geo,
    total,
    piece_out,
    piece_in,
    halo_send,
    halo_recv,
    own_send,
    own_recv,
    tile_send,
    tile_recv,
    image_send,
    image_recv,
    local,
):
    plane, wire, tick = lax.axis_index("plane"), lax.axis_index("wire"), lax.axis_index("tick")
    me = plane * 4 + wire
    half, inner = wire // 2, lax.rem(wire, 2)
    spot = plane * 2 + inner
    whole = jnp.logical_or(wire == 1, wire == 2)
    split = jnp.logical_not(whole)
    mine = plane * 2 + half
    up_t, down_t = lax.rem(tick + 1, 16), lax.rem(tick + 15, 16)
    up_w, down_w = lax.rem(wire + 1, 4), lax.rem(wire + 3, 4)

    def member(m):
        return (m // 4, lax.rem(m, 4), tick)

    barrier = pltpu.get_barrier_semaphore()

    def greet(r, carry):
        pl.semaphore_signal(barrier, inc=1, device_id=member(lax.rem(me + r, N)), device_id_type=MESH)
        return carry

    for w in (wire, up_w, down_w):
        for t in (up_t, down_t):
            pl.semaphore_signal(barrier, inc=1, device_id=(plane, w, t), device_id_type=MESH)
    lax.fori_loop(1, N, greet, 0)

    raw_copy = pltpu.make_async_copy(raw_hbm, raw_ref, local.at[3])
    raw_copy.start()
    geo_copy = pltpu.make_async_copy(geo_ref, geo, local.at[0])
    geo_copy.start()
    taps[...] = jnp.zeros((24, 2 * TB), F32)
    taps[0:21, :] = taps_ref[...].astype(F32)
    roi_ref[...] = jnp.full((8, TB), -1, jnp.int32)
    roi_ref[0:1, 0:102] = block_ref[...]
    roi_ref[1:2, 0:102] = owner_ref[...]

    row = lax.broadcasted_iota(jnp.int32, (256, 256), 0)
    col = lax.broadcasted_iota(jnp.int32, (256, 256), 1)
    diag = jnp.where(row == col, mask_ref[...].astype(F32), 0.0).astype(BF16)
    mask_col[...] = jnp.dot(diag, jnp.ones((256, TB), BF16), preferred_element_type=F32)

    ids = roi_ref[0:1, :]
    owner = roi_ref[1:2, :]
    tick_hit = jnp.where(
        lax.broadcasted_iota(jnp.int32, (N, TB), 0) == lax.rem(ids, 16), 1.0, 0.0
    ).astype(BF16)
    wire_hit = jnp.where(
        lax.broadcasted_iota(jnp.int32, (256, TB), 0) // 32 == ids // 16, (owner + 1).astype(F32), 0.0
    ).astype(BF16)
    table = lax.dot_general(tick_hit, wire_hit, (((1,), (1,)), ((), ())), preferred_element_type=F32)
    for m in range(N):
        for side in range(2):
            own_out[m, side : side + 1, :] = table[m : m + 1, side * TB : (side + 1) * TB]
        own_out[m, 2:8, :] = jnp.zeros((6, TB), F32)

    raw_copy.wait()
    for side, start in ((0, 0), (1, 15 * TB)):
        edge_t[side] = (raw_ref[:, start : start + TB].astype(F32) * mask_col[...]).astype(BF16)
    for side, start in ((0, 0), (1, 240)):
        for j in range(N):
            cols = slice(j * TB, (j + 1) * TB)
            edge_w[side, :, cols] = (
                raw_ref[start : start + 16, cols].astype(F32) * mask_col[start : start + 16, :]
            ).astype(BF16)

    pl.semaphore_wait(barrier, 21)

    first, last = slice(0, TB), slice(15 * TB, 16 * TB)
    halo_copies = [
        pltpu.make_async_remote_copy(
            src_ref=src,
            dst_ref=dst,
            send_sem=halo_send.at[i],
            recv_sem=halo_recv.at[i],
            device_id=(plane, w, t),
            device_id_type=MESH,
        )
        for i, (src, dst, w, t) in enumerate(
            (
                (edge_t.at[1], halo_t.at[0], wire, up_t),
                (edge_t.at[0], halo_t.at[1], wire, down_t),
                (edge_w.at[1], halo_w.at[0], up_w, tick),
                (edge_w.at[0], halo_w.at[1], down_w, tick),
                (edge_w.at[1, :, last], halo_c.at[0], up_w, up_t),
                (edge_w.at[1, :, first], halo_c.at[1], up_w, down_t),
                (edge_w.at[0, :, last], halo_c.at[2], down_w, up_t),
                (edge_w.at[0, :, first], halo_c.at[3], down_w, down_t),
            )
        )
    ]
    for copy in halo_copies:
        copy.start()

    def to_whole(a, src, dst, send, receive):
        return pltpu.make_async_remote_copy(
            src_ref=src(a),
            dst_ref=dst(half, spot),
            send_sem=send.at[a],
            recv_sem=receive.at[half, spot],
            device_id=(a // 2, 1 + lax.rem(a, 2), tick),
            device_id_type=MESH,
        )

    def to_split(p, h, src, dst, send, receive):
        return pltpu.make_async_remote_copy(
            src_ref=src(8 + 2 * p + h),
            dst_ref=dst(h, spot),
            send_sem=send.at[8 + 2 * p + h],
            recv_sem=receive.at[h, spot],
            device_id=(p, 3 * half, tick),
            device_id_type=MESH,
        )

    def exchange(act, *refs):
        def wholes(r, carry):
            act(to_whole(lax.rem(mine + r, 8), *refs))
            return carry

        def splits(r, carry):
            for h in range(2):
                act(to_split(lax.rem(plane + r, 4), h, *refs))
            return carry

        lax.fori_loop(1, 8, wholes, 0)
        lax.fori_loop(1, 4, splits, 0)

        @pl.when(split)
        def _():
            act(to_whole(mine, *refs))

        @pl.when(whole)
        def _():
            for h in range(2):
                act(to_split(plane, h, *refs))

    def begin(copy):
        copy.start()

    def wait_send(copy):
        copy.wait_send()

    def arrival(h, other, dst, receive):
        return pltpu.make_async_remote_copy(
            src_ref=dst(h, other),
            dst_ref=dst(h, other),
            send_sem=receive.at[h, other],
            recv_sem=receive.at[h, other],
            device_id=(other // 2, 2 * jnp.where(whole, h, half) + lax.rem(other, 2), tick),
            device_id_type=MESH,
        )

    def wait_half(h, second, dst, receive):
        def one(r, carry):
            arrival(h, lax.rem(spot + r, 8), dst, receive).wait_recv()
            return carry

        lax.fori_loop(1, 8, one, 0)
        if second:

            @pl.when(whole)
            def _():
                arrival(h, spot, dst, receive).wait_recv()

    own_refs = (lambda j: own_out.at[j], lambda h, i: own_in.at[h, i], own_send, own_recv)
    exchange(begin, *own_refs)

    @pl.when(whole)
    def _():
        own_in[half, spot] = own_out[mine]

    @pl.when(split)
    def _():
        for h in range(2):
            own_in[h, spot] = own_out[8 + 2 * plane + h]

    build_bands(taps, band)

    def spread(i, carry):
        wires = pl.ds(pl.multiple_of(i * 16, 16), 16)
        keep = mask_col[wires, :]
        for j in range(N):
            piece = raw_ref[wires, j * TB : (j + 1) * TB].astype(F32) * keep
            tall[pl.ds((i + 1) * 288 + j + 1, 16, stride=18), :] = piece
        return carry

    lax.fori_loop(0, 16, spread, 0)

    geo_copy.wait()
    row = lax.broadcasted_iota(jnp.int32, (TB, TB), 0)
    col = lax.broadcasted_iota(jnp.int32, (TB, TB), 1)
    eye = jnp.where(row == col, 1.0, 0.0).astype(BF16)

    def turn(s, carry):
        rows = pl.ds(pl.multiple_of(s * 256, 256), 256)
        geo_t[s] = lax.dot_general(
            eye, geo[rows, :], (((1,), (1,)), ((), ())), preferred_element_type=F32
        ).astype(BF16)
        return carry

    lax.fori_loop(0, N, turn, 0)

    tick_ok = [jnp.where(tick == 0, 0.0, 1.0), jnp.where(tick == 15, 0.0, 1.0)]
    wire_ok = [jnp.where(wire == 0, 0.0, 1.0), jnp.where(wire == 3, 0.0, 1.0)]

    def window(i, carry):
        for u in range(8):
            slot = i * 8 + u
            for piece in range(3):
                shifted[piece, slot] = tall[pl.ds(slot * 18 + piece, 16), :].astype(BF16)
        return carry

    for side in range(2):
        halo_copies[side].wait_recv()

    def spread_ticks(i, carry):
        wires = pl.ds(pl.multiple_of(i * 16, 16), 16)
        for side, j in ((0, 0), (1, 17)):
            tall[pl.ds((i + 1) * 288 + j, 16, stride=18), :] = (
                halo_t[side, wires, :].astype(F32) * tick_ok[side]
            )
        return carry

    lax.fori_loop(0, 16, spread_ticks, 0)
    lax.fori_loop(2, 34, window, 0)

    def run_chunk(c):
        base = c * CHUNK
        lhs = jnp.concatenate(
            [
                shifted[piece, pl.ds(base + 6 + 2 * m, CHUNK + 1)].reshape((CHUNK + 1) * 16, TB)
                for m in range(11)
                for piece in range(3)
            ],
            axis=1,
        )
        both = jnp.dot(lhs, band[...], preferred_element_type=F32)
        sums[...] = both[:ROWS, :TB] + both[16:, TB:]
        for j in range(N):
            for b in range(CHUNK // 16):
                start = pl.multiple_of(base + b * 16, 16)
                sig[j, pl.ds(start, 16), :] = sums[pl.ds(b * 256 + j, 16, stride=16), :].astype(BF16)
        part = pl.ds(pl.multiple_of(base, CHUNK), CHUNK)

        exchange(begin, lambda j: sig.at[j, part], lambda h, i: recv.at[h, i, part], tile_send, tile_recv)

    def middle(i, carry):
        run_chunk(i + 1)
        return carry

    lax.fori_loop(0, 2, middle, 0)

    for copy in halo_copies[2:]:
        copy.wait_recv()
    for side, base in ((0, 0), (1, 272 * 18)):
        for j in range(N):
            tall[pl.ds(base + j + 1, 16, stride=18), :] = (
                halo_w[side, :, j * TB : (j + 1) * TB].astype(F32) * wire_ok[side]
            )
        for t, j in ((0, 0), (1, 17)):
            tall[pl.ds(base + j, 16, stride=18), :] = (
                halo_c[side * 2 + t].astype(F32) * wire_ok[side] * tick_ok[t]
            )
    lax.fori_loop(0, 2, window, 0)
    lax.fori_loop(34, 36, window, 0)

    def outer(i, carry):
        run_chunk(i * 3)
        return carry

    lax.fori_loop(0, 2, outer, 0)

    def store_signal(j, carry):
        pltpu.make_async_copy(
            sig.at[j], signal_ref.at[:, pl.ds(pl.multiple_of(j * TB, TB), TB)], local.at[1]
        ).start()
        return carry

    lax.fori_loop(0, N, store_signal, 0)

    @pl.when(whole)
    def _():
        recv[half, spot] = sig[mine]

    @pl.when(split)
    def _():
        for h in range(2):
            recv[h, spot] = sig[8 + 2 * plane + h]

    first_half = jnp.where(whole, half, 0)
    own_dst, tile_dst = own_refs[1], lambda h, i: recv.at[h, i]
    wait_half(first_half, False, own_dst, own_recv)
    wait_half(1 - first_half, True, own_dst, own_recv)

    def mask_geo(i, carry):
        for h in range(2):
            wires = jnp.where(whole, h, half)
            s = (i // 2) * 4 + 2 * wires + lax.rem(i, 2)
            for side in range(2):
                owners = own_in[h, i, side : side + 1, :]
                part = geo_t[s, :, side * TB : (side + 1) * TB]
                cols = pl.ds(pl.multiple_of(i * 256 + side * TB, TB), TB)
                for o in range(N):
                    keep = jnp.where(owners == o + 1, 1.0, 0.0).astype(BF16)
                    masked_geo[h, o, :, cols] = part * keep
        return carry

    lax.fori_loop(0, 8, mask_geo, 0)

    def image_slot(p, w, h, k):
        outer = jnp.logical_or(w == 0, w == 3)
        return jnp.where(outer, 8 + (2 * p + k) * 2 + h, 2 * p + h)

    def image_copy(k, o):
        slot = image_slot(plane, wire, half, k)
        return pltpu.make_async_remote_copy(
            src_ref=piece_out.at[k, o],
            dst_ref=piece_in.at[slot],
            send_sem=image_send.at[k, o],
            recv_sem=image_recv.at[slot],
            device_id=member(o),
            device_id_type=MESH,
        )

    both_halves = jnp.where(whole, 1.0, 0.0)
    for turn_now in range(2):
        h = first_half if turn_now == 0 else 1 - first_half
        k = 0 if turn_now == 0 else jnp.where(whole, 0, 1)
        wait_half(h, turn_now == 1, tile_dst, tile_recv)
        tiles = recv[h].reshape(2048, TB)
        for quarter in range(4):
            members = [lax.rem(me + 1 + 4 * quarter + i, N) for i in range(4)]
            lhs = jnp.concatenate([masked_geo[h, o] for o in members], axis=0)
            part = jnp.dot(lhs, tiles, preferred_element_type=F32)
            for i, o in enumerate(members):
                now = part[i * TB : (i + 1) * TB]
                if turn_now == 0:
                    total[o] = now
                else:
                    now = now + total[o] * both_halves

                def send_piece():
                    piece_out[k, o] = now.astype(BF16)
                    if quarter * 4 + i < N - 1:
                        image_copy(k, o).start()
                    else:
                        piece_in[image_slot(plane, wire, half, k)] = piece_out[k, o]

                if turn_now == 0:
                    pl.when(split)(send_piece)
                else:
                    send_piece()

    for copy in halo_copies:
        copy.wait_send()
    exchange(wait_send, *own_refs)
    exchange(wait_send, lambda j: sig.at[j], tile_dst, tile_send, tile_recv)
    pltpu.make_async_copy(signal_ref, signal_ref, local.at[1]).wait()

    def wait_image_send(k):
        def one(r, carry):
            image_copy(k, lax.rem(me + r, N)).wait_send()
            return carry

        lax.fori_loop(1, N, one, 0)

    wait_image_send(0)

    @pl.when(split)
    def _():
        wait_image_send(1)

    def image_arrival(slot):
        return pltpu.make_async_remote_copy(
            src_ref=piece_in.at[slot],
            dst_ref=piece_in.at[slot],
            send_sem=image_recv.at[slot],
            recv_sem=image_recv.at[slot],
            device_id=(plane, up_w, tick),
            device_id_type=MESH,
        )

    def whole_images(r, carry):
        image_arrival(lax.rem(mine + r, 8)).wait_recv()
        return carry

    def split_images(r, carry):
        for k in range(2):
            for h in range(2):
                image_arrival(8 + (2 * lax.rem(plane + r, 4) + k) * 2 + h).wait_recv()
        return carry

    lax.fori_loop(1, 8, whole_images, 0)
    lax.fori_loop(1, 4, split_images, 0)
    for k in range(2):
        image_arrival(8 + (2 * plane + k) * 2 + 1 - half).wait_recv()

    @pl.when(split)
    def _():
        image_arrival(mine).wait_recv()

    @pl.when(whole)
    def _():
        for k in range(2):
            image_arrival(8 + (2 * plane + k) * 2 + half).wait_recv()

    image_ref[...] = piece_in[...]


def finish_kernel(signal_ref, piece_ref, signal_out, image_ref, held, sem):
    parts = [pl.ds(i * 64, 64) for i in range(4)]
    loads = [pltpu.make_async_copy(signal_ref.at[p], held.at[p], sem.at[0, i]) for i, p in enumerate(parts)]
    stores = [pltpu.make_async_copy(held.at[p], signal_out.at[p], sem.at[1, i]) for i, p in enumerate(parts)]
    for load in loads:
        load.start()
    for load, store in zip(loads, stores):
        load.wait()
        store.start()
    for j in range(8):
        image_ref[:, j * TB : (j + 1) * TB] = piece_ref[j].astype(F32)
        image_ref[:, (8 + j) * TB : (9 + j) * TB] = piece_ref[8 + 2 * j].astype(F32) + piece_ref[
            9 + 2 * j
        ].astype(F32)
    for store in stores:
        store.wait()


def finish(signal, pieces):
    return pl.pallas_call(
        finish_kernel,
        out_shape=(
            jax.ShapeDtypeStruct((256, 2048), BF16),
            jax.ShapeDtypeStruct((TB, 2048), F32),
        ),
        in_specs=[ANY, VMEM],
        out_specs=(ANY, VMEM),
        scratch_shapes=[pltpu.VMEM((256, 2048), BF16), pltpu.SemaphoreType.DMA((2, 4))],
        name="finish",
    )(signal, pieces)


def fused(raw, mask, taps, blocks, owners, geo):
    dma = pltpu.SemaphoreType.DMA
    return pl.pallas_call(
        kernel,
        out_shape=(
            jax.ShapeDtypeStruct((256, 2048), BF16),
            jax.ShapeDtypeStruct((24, TB, TB), BF16),
        ),
        in_specs=[ANY, VMEM, VMEM, VMEM, VMEM, ANY],
        out_specs=(ANY, VMEM),
        scratch_shapes=[
            pltpu.VMEM((256, 2048), BF16),
            pltpu.VMEM((24, 2 * TB), F32),
            pltpu.VMEM((8, TB), jnp.int32),
            pltpu.VMEM((2, 256, TB), BF16),
            pltpu.VMEM((2, 16, 2048), BF16),
            pltpu.VMEM((2, 256, TB), BF16),
            pltpu.VMEM((2, 16, 2048), BF16),
            pltpu.VMEM((4, 16, TB), BF16),
            pltpu.VMEM((256, TB), F32),
            pltpu.VMEM((288 * 18, TB), F32),
            pltpu.VMEM((3, 288, 16, TB), BF16),
            pltpu.VMEM((33 * TB, 2 * TB), BF16),
            pltpu.VMEM((ROWS, TB), F32),
            pltpu.VMEM((N, 256, TB), BF16),
            pltpu.VMEM((2, 8, 256, TB), BF16),
            pltpu.VMEM((N, 8, TB), F32),
            pltpu.VMEM((2, 8, 8, TB), F32),
            pltpu.VMEM((4096, TB), BF16),
            pltpu.VMEM((N, TB, 256), BF16),
            pltpu.VMEM((2, N, TB, 2048), BF16),
            pltpu.VMEM((N, TB, TB), F32),
            pltpu.VMEM((2, N, TB, TB), BF16),
            pltpu.VMEM((24, TB, TB), BF16),
            dma((8,)),
            dma((8,)),
            dma((N,)),
            dma((2, 8)),
            dma((N,)),
            dma((2, 8)),
            dma((2, N)),
            dma((24,)),
            dma((4,)),
        ],
        compiler_params=pltpu.CompilerParams(
            vmem_limit_bytes=56 << 20, collective_id=0, has_side_effects=True
        ),
        name="fused",
    )(raw, mask, taps, blocks, owners, geo)


def shards(raw, chan_mask, kernel_rows, geometry, roi_block, roi_owner):
    signal, pieces = fused(
        raw,
        chan_mask.reshape(1, 256),
        kernel_rows[0],
        roi_block.reshape(1, -1),
        roi_owner.reshape(1, -1),
        geometry.reshape(4096, TB),
    )
    return finish(signal, pieces)


def solution(mesh):
    in_specs = (
        P(("plane", "wire"), "tick"),
        P(("plane", "wire")),
        P("plane", None, None),
        P(),
        P(("plane", "wire", "tick")),
        P(("plane", "wire", "tick")),
    )
    out_specs = (P(("plane", "wire"), "tick"), P(("plane", "wire"), "tick"))
    return jax.shard_map(shards, mesh=mesh, in_specs=in_specs, out_specs=out_specs, check_vma=False)
```

```python
import jax
import jax.numpy as jnp
from jax import lax
from jax.experimental import pallas as pl
from jax.experimental.pallas import tpu as pltpu
from jax.sharding import PartitionSpec as P

TB = 128
N = 16
CHUNK = 64
ROWS = CHUNK * 16
BLOCKS = 22
UNROLL = BLOCKS
LIMIT = 56 << 20
MESH = pl.DeviceIdType.MESH
VMEM = pl.BlockSpec(memory_space=pltpu.VMEM)
ANY = pl.BlockSpec(memory_space=pl.ANY)
HBM = pl.BlockSpec(memory_space=pltpu.HBM)
BF16 = jnp.bfloat16
F32 = jnp.float32


def row_of(ref, index, size):
    return ref.at[pl.ds(pl.multiple_of(index, size), size)]


def build_bands(taps_ref, band_ref):
    row = lax.broadcasted_iota(jnp.int32, (TB, TB), 0)
    col = lax.broadcasted_iota(jnp.int32, (TB, TB), 1)
    upper = col >= row
    zero = jnp.zeros((TB, TB), F32)

    def pair(m, carry):
        for p in range(2):
            taps = taps_ref[pl.ds(2 * m + p, 1), :]
            low, high = [
                pltpu.roll(
                    jnp.broadcast_to(taps[:, half * TB : (half + 1) * TB], (TB, TB)),
                    0,
                    1,
                    stride=1,
                    stride_axis=0,
                )
                for half in range(2)
            ]
            pieces = (
                jnp.where(upper, zero, high),
                jnp.where(upper, high, low),
                jnp.where(upper, low, zero),
            )
            for piece in range(3):
                start = pl.multiple_of((m * 3 + piece) * TB, TB)
                band_ref[pl.ds(start, TB), p * TB : (p + 1) * TB] = pieces[piece].astype(BF16)
        return carry

    lax.fori_loop(0, 11, pair, 0)


def kernel(
    raw_hbm,
    mask_ref,
    taps_ref,
    block_ref,
    owner_ref,
    geo_ref,
    signal_ref,
    image_ref,
    raw_ref,
    taps,
    roi_ref,
    edge_t,
    edge_w,
    halo_t,
    halo_w,
    halo_c,
    mask_col,
    tall,
    shifted,
    band,
    sums,
    sig,
    recv_0,
    recv_1,
    own_out,
    own_in,
    geo,
    plan_v,
    plan,
    runs,
    piece_out,
    piece_in,
    halo_send,
    halo_recv,
    own_send,
    own_recv,
    tile_send,
    tile_recv,
    image_send,
    image_recv,
    local,
):
    plane, wire, tick = lax.axis_index("plane"), lax.axis_index("wire"), lax.axis_index("tick")
    me = plane * 4 + wire
    recv = (recv_0, recv_1)
    half, inner = wire // 2, lax.rem(wire, 2)
    spot = plane * 2 + inner
    whole = jnp.logical_or(wire == 1, wire == 2)
    split = jnp.logical_not(whole)
    mine = plane * 2 + half
    up_t, down_t = lax.rem(tick + 1, 16), lax.rem(tick + 15, 16)
    up_w, down_w = lax.rem(wire + 1, 4), lax.rem(wire + 3, 4)

    def member(m):
        return (m // 4, lax.rem(m, 4), tick)

    barrier = pltpu.get_barrier_semaphore()

    def greet(r, carry):
        pl.semaphore_signal(barrier, inc=1, device_id=member(lax.rem(me + r, N)), device_id_type=MESH)
        return carry

    has = {"t+": tick < 15, "t-": tick > 0, "w+": wire < 3, "w-": wire > 0}

    def when_all(keys, action):
        test = has[keys[0]]
        for key in keys[1:]:
            test = jnp.logical_and(test, has[key])
        pl.when(test)(action)
        return test

    for t_key, t in (("t+", up_t), ("t-", down_t)):
        for w_keys, w in (((), wire), (("w+",), up_w), (("w-",), down_w)):

            def greet_side():
                pl.semaphore_signal(barrier, inc=1, device_id=(plane, w, t), device_id_type=MESH)

            when_all((t_key, *w_keys), greet_side)
    lax.fori_loop(1, N, greet, 0)

    raw_copy = pltpu.make_async_copy(raw_hbm, raw_ref, local.at[3])
    raw_copy.start()
    geo_copy = pltpu.make_async_copy(geo_ref, geo, local.at[0])
    geo_copy.start()
    taps[...] = jnp.zeros((24, 2 * TB), F32)
    taps[0:21, :] = taps_ref[...].astype(F32)
    roi_ref[...] = jnp.full((8, TB), -1, jnp.int32)
    roi_ref[0:1, 0:102] = block_ref[...]
    roi_ref[1:2, 0:102] = owner_ref[...]

    row = lax.broadcasted_iota(jnp.int32, (256, 256), 0)
    col = lax.broadcasted_iota(jnp.int32, (256, 256), 1)
    diag = jnp.where(row == col, mask_ref[...].astype(F32), 0.0).astype(BF16)
    mask_col[...] = jnp.dot(diag, jnp.ones((256, TB), BF16), preferred_element_type=F32)

    r = lax.broadcasted_iota(jnp.int32, (TB, TB), 0)
    hit = jnp.where(roi_ref[0:1, :] == lax.rem(r, 8) * 16 + r // 8, roi_ref[1:2, :] + 1, 0)
    table = jnp.dot(hit.astype(F32).astype(BF16), jnp.ones((TB, TB), BF16), preferred_element_type=F32)
    own_out[...] = table.reshape(N, 8, TB)

    raw_copy.wait()
    for side, start in ((0, 0), (1, 15 * TB)):
        edge_t[side] = (raw_ref[:, start : start + TB].astype(F32) * mask_col[...]).astype(BF16)
    for side, start in ((0, 0), (1, 240)):
        for j in range(N):
            cols = slice(j * TB, (j + 1) * TB)
            edge_w[side, :, cols] = (
                raw_ref[start : start + 16, cols].astype(F32) * mask_col[start : start + 16, :]
            ).astype(BF16)

    ticks_near = (tick < 15).astype(jnp.int32) + (tick > 0).astype(jnp.int32)
    wires_near = 1 + (wire < 3).astype(jnp.int32) + (wire > 0).astype(jnp.int32)
    pl.semaphore_wait(barrier, 15 + ticks_near * wires_near)

    first, last = slice(0, TB), slice(15 * TB, 16 * TB)
    halo_copies = [
        pltpu.make_async_remote_copy(
            src_ref=src,
            dst_ref=dst,
            send_sem=halo_send.at[i],
            recv_sem=halo_recv.at[i],
            device_id=(plane, w, t),
            device_id_type=MESH,
        )
        for i, (src, dst, w, t) in enumerate(
            (
                (edge_t.at[1], halo_t.at[0], wire, up_t),
                (edge_t.at[0], halo_t.at[1], wire, down_t),
                (edge_w.at[1], halo_w.at[0], up_w, tick),
                (edge_w.at[0], halo_w.at[1], down_w, tick),
                (edge_w.at[1, :, last], halo_c.at[0], up_w, up_t),
                (edge_w.at[1, :, first], halo_c.at[1], up_w, down_t),
                (edge_w.at[0, :, last], halo_c.at[2], down_w, up_t),
                (edge_w.at[0, :, first], halo_c.at[3], down_w, down_t),
            )
        )
    ]
    outward = (("t+",), ("t-",), ("w+",), ("w-",), ("w+", "t+"), ("w+", "t-"), ("w-", "t+"), ("w-", "t-"))
    inward = (("t-",), ("t+",), ("w-",), ("w+",), ("w-", "t-"), ("w-", "t+"), ("w+", "t-"), ("w+", "t+"))
    landing = [halo_t.at[0], halo_t.at[1], halo_w.at[0], halo_w.at[1]] + [halo_c.at[i] for i in range(4)]
    for keys, copy in zip(outward, halo_copies):
        when_all(keys, copy.start)

    def take_halo(i):
        test = when_all(inward[i], halo_copies[i].wait_recv)

        @pl.when(jnp.logical_not(test))
        def _():
            landing[i][...] = jnp.zeros(landing[i].shape, BF16)

    def to_whole(r, turn, src, dst, send, receive):
        a = lax.rem(mine + r, 8)
        return pltpu.make_async_remote_copy(
            src_ref=src(a),
            dst_ref=dst(turn, spot),
            send_sem=send.at[a],
            recv_sem=receive.at[turn, spot],
            device_id=(a // 2, 1 + lax.rem(a, 2), tick),
            device_id_type=MESH,
        )

    def to_split(p, h, src, dst, send, receive):
        return pltpu.make_async_remote_copy(
            src_ref=src(8 + 2 * p + h),
            dst_ref=dst(h, spot),
            send_sem=send.at[8 + 2 * p + h],
            recv_sem=receive.at[h, spot],
            device_id=(p, 3 * half, tick),
            device_id_type=MESH,
        )

    def exchange(act, *refs):
        def across(i, carry):
            act(to_whole(2 * i + 1, 1, *refs))
            return carry

        def within(i, carry):
            act(to_whole(2 * i, 0, *refs))
            return carry

        def splits(r, carry):
            for h in range(2):
                act(to_split(lax.rem(plane + r, 4), h, *refs))
            return carry

        lax.fori_loop(0, 4, across, 0)
        lax.fori_loop(1, 4, within, 0)
        lax.fori_loop(1, 4, splits, 0)

        @pl.when(split)
        def _():
            act(to_whole(0, 0, *refs))

        @pl.when(whole)
        def _():
            for h in range(2):
                act(to_split(plane, h, *refs))

    def begin(copy):
        copy.start()

    def wait_send(copy):
        copy.wait_send()

    def side_of(turn):
        return jnp.where(whole, 1 - half, half) if turn else half

    def arrival(h, other, dst, receive):
        return pltpu.make_async_remote_copy(
            src_ref=dst(h, other),
            dst_ref=dst(h, other),
            send_sem=receive.at[h, other],
            recv_sem=receive.at[h, other],
            device_id=(other // 2, 2 * side_of(h) + lax.rem(other, 2), tick),
            device_id_type=MESH,
        )

    def wait_half(h, second, dst, receive):
        def one(r, carry):
            arrival(h, lax.rem(spot + r, 8), dst, receive).wait_recv()
            return carry

        lax.fori_loop(1, 8, one, 0)
        if second:

            @pl.when(whole)
            def _():
                arrival(h, spot, dst, receive).wait_recv()

    own_refs = (lambda j: own_out.at[j], lambda h, i: own_in.at[h, i], own_send, own_recv)
    exchange(begin, *own_refs)

    @pl.when(whole)
    def _():
        own_in[0, spot] = own_out[mine]

    @pl.when(split)
    def _():
        for h in range(2):
            own_in[h, spot] = own_out[8 + 2 * plane + h]

    build_bands(taps, band)

    def spread(i, carry):
        wires = pl.ds(pl.multiple_of(i * 16, 16), 16)
        keep = mask_col[wires, :]
        for j in range(N):
            piece = raw_ref[wires, j * TB : (j + 1) * TB].astype(F32) * keep
            tall[pl.ds((i + 1) * 288 + j + 1, 16, stride=18), :] = piece
        return carry

    lax.fori_loop(0, 16, spread, 0)

    def window(i, carry):
        for u in range(8):
            slot = i * 8 + u
            for piece in range(3):
                shifted[piece, slot] = tall[pl.ds(slot * 18 + piece, 16), :].astype(BF16)
        return carry

    for i in (0, 1):
        take_halo(i)

    def spread_ticks(i, carry):
        wires = pl.ds(pl.multiple_of(i * 16, 16), 16)
        for side, j in ((0, 0), (1, 17)):
            tall[pl.ds((i + 1) * 288 + j, 16, stride=18), :] = halo_t[side, wires, :].astype(F32)
        return carry

    lax.fori_loop(0, 16, spread_ticks, 0)
    lax.fori_loop(2, 34, window, 0)

    def run_chunk(c):
        base = c * CHUNK
        lhs = jnp.concatenate(
            [
                shifted[piece, pl.ds(base + 6 + 2 * m, CHUNK + 1)].reshape((CHUNK + 1) * 16, TB)
                for m in range(11)
                for piece in range(3)
            ],
            axis=1,
        )
        both = jnp.dot(lhs, band[...], preferred_element_type=F32)
        sums[...] = both[:ROWS, :TB] + both[16:, TB:]
        for j in range(N):
            for b in range(CHUNK // 16):
                sig[j, c * 2 + b // 2, (b % 2) * 16 : (b % 2) * 16 + 16, :] = sums[pl.ds(b * 256 + j, 16, stride=16), :].astype(BF16)

        exchange(
            begin,
            lambda j: sig.at[j, pl.ds(c * 2, 2)],
            lambda h, i: recv[h].at[pl.ds(i * 8 + c * 2, 2)],
            tile_send,
            tile_recv,
        )

    def middle(i, carry):
        run_chunk(i + 1)
        return carry

    lax.fori_loop(0, 2, middle, 0)

    for i in range(2, 8):
        take_halo(i)
    for side, base in ((0, 0), (1, 272 * 18)):
        for j in range(N):
            tall[pl.ds(base + j + 1, 16, stride=18), :] = halo_w[side, :, j * TB : (j + 1) * TB].astype(F32)
        for t, j in ((0, 0), (1, 17)):
            tall[pl.ds(base + j, 16, stride=18), :] = halo_c[side * 2 + t].astype(F32)
    lax.fori_loop(0, 2, window, 0)
    lax.fori_loop(34, 36, window, 0)

    def outer(i, carry):
        run_chunk(i * 3)
        return carry

    lax.fori_loop(0, 2, outer, 0)

    def store_signal(j, carry):
        pltpu.make_async_copy(
            sig.at[j], signal_ref.at[:, :, pl.ds(pl.multiple_of(j * TB, TB), TB)], local.at[1]
        ).start()
        return carry

    lax.fori_loop(0, N, store_signal, 0)

    @pl.when(whole)
    def _():
        recv[0][pl.ds(spot * 8, 8)] = sig[mine]

    @pl.when(split)
    def _():
        for h in range(2):
            recv[h][pl.ds(spot * 8, 8)] = sig[8 + 2 * plane + h]

    own_dst, tile_dst = own_refs[1], lambda h, i: recv[h].at[pl.ds(i * 8, 8)]
    wait_half(0, False, own_dst, own_recv)
    wait_half(1, True, own_dst, own_recv)

    tile = lax.broadcasted_iota(jnp.int32, (64, TB), 0)
    lane = lax.broadcasted_iota(jnp.int32, (64, TB), 1)
    place = lax.broadcasted_iota(jnp.int32, (64, 2 * TB), 1).astype(F32)
    before = (lax.broadcasted_iota(jnp.int32, (64, 64), 1) < lax.broadcasted_iota(jnp.int32, (64, 64), 0)).astype(
        F32
    )
    lower = (lax.broadcasted_iota(jnp.int32, (TB, TB), 0) < lax.broadcasted_iota(jnp.int32, (TB, TB), 1)).astype(
        F32
    )
    for h in range(2):
        side = side_of(h)
        georow = ((tile // 16) * 4 + 2 * side + lax.rem(tile // 8, 2)) * 8 + lax.rem(tile, 8)
        wanted = own_in[h].reshape(64, TB)
        member_of = jnp.where(wanted == (lane + 1).astype(F32), 1.0, 0.0)
        rank = jnp.dot(before.astype(BF16), member_of.astype(BF16), preferred_element_type=F32)
        count = jnp.sum(member_of, axis=0, keepdims=True)
        blocks = jnp.floor((count + 7.0) * 0.125)
        opening = jnp.dot(
            jnp.broadcast_to(blocks, (8, TB)).astype(BF16), lower.astype(BF16), preferred_element_type=F32
        )[0:1, :]
        found = jnp.sum(member_of, axis=1, keepdims=True)
        spot_of = jnp.sum(member_of * (opening * 8.0 + rank), axis=1, keepdims=True) - (1.0 - found)
        rank_of = jnp.sum(member_of * rank, axis=1, keepdims=True)
        here = jnp.where(spot_of == place, 1.0, 0.0)
        tile_f, geo_f = tile[:, 0:1].astype(F32), georow[:, 0:1].astype(F32)
        plan_v[h, 0:1, :] = (64.0 + jnp.sum(here * (tile_f - 64.0), axis=0, keepdims=True)).astype(jnp.int32)
        plan_v[h, 1:2, :] = jnp.sum(here * geo_f, axis=0, keepdims=True).astype(jnp.int32)
        again = jnp.where(spot_of == place * 8.0, 1.0, 0.0) * jnp.where(rank_of > 0.0, 1.0, 0.0)
        plan_v[h, 2:3, :] = jnp.sum(again, axis=0, keepdims=True).astype(jnp.int32)
        closing = jnp.where(count > 0.0, opening + blocks - 1.0, float(BLOCKS))
        plan_v[h, 3:4, 0:TB] = closing.astype(jnp.int32)
        plan_v[h, 3:4, TB : 2 * TB] = closing.astype(jnp.int32)
        plan_v[h, 4:8, :] = jnp.zeros((4, 2 * TB), jnp.int32)
        recv[h][64] = jnp.zeros((32, TB), BF16)
        runs[h, BLOCKS] = jnp.zeros((TB, TB), F32)
    plan_copy = pltpu.make_async_copy(plan_v, plan, local.at[2])
    plan_copy.start()
    geo_copy.wait()
    plan_copy.wait()

    def image_slot(p, w, h, k):
        outer = jnp.logical_or(w == 0, w == 3)
        return jnp.where(outer, 8 + (2 * p + k) * 2 + h, 2 * p + h)

    def image_copy(k, o):
        slot = image_slot(plane, wire, half, k)
        return pltpu.make_async_remote_copy(
            src_ref=piece_out.at[k, o],
            dst_ref=piece_in.at[slot],
            send_sem=image_send.at[k, o],
            recv_sem=image_recv.at[slot],
            device_id=member(o),
            device_id_type=MESH,
        )

    both_halves = jnp.where(whole, 1.0, 0.0)
    for h in range(2):
        k = 0 if h == 0 else jnp.where(whole, 0, 1)
        wait_half(h, h == 1, tile_dst, tile_recv)

        def block(b, run):
            lhs = jnp.concatenate([geo[jnp.clip(plan[h, 1, b * 8 + i], 0, TB - 1)] for i in range(8)], axis=0)
            rhs = jnp.concatenate([recv[h][jnp.clip(plan[h, 0, b * 8 + i], 0, 64)] for i in range(8)], axis=0)
            part = lax.dot_general(lhs, rhs, (((0,), (0,)), ((), ())), preferred_element_type=F32)
            run = run * plan[h, 2, b].astype(F32) + part
            runs[h, b] = run
            return run

        lax.fori_loop(0, BLOCKS, block, jnp.zeros((TB, TB), F32), unroll=UNROLL)

        for i in range(N):
            o = lax.rem(me + 1 + i, N)

            def send_piece():
                now = runs[h, jnp.clip(plan[h, 3, o], 0, BLOCKS)]
                if h == 1:
                    now = now + runs[0, jnp.clip(plan[0, 3, o], 0, BLOCKS)] * both_halves
                piece_out[k, o] = now.astype(BF16)
                if i < N - 1:
                    image_copy(k, o).start()
                else:
                    piece_in[image_slot(plane, wire, half, k)] = piece_out[k, o]

            if h == 0:
                pl.when(split)(send_piece)
            else:
                send_piece()

    for keys, copy in zip(outward, halo_copies):
        when_all(keys, copy.wait_send)
    exchange(wait_send, *own_refs)
    exchange(wait_send, lambda j: sig.at[j], tile_dst, tile_send, tile_recv)
    pltpu.make_async_copy(signal_ref, signal_ref, local.at[1]).wait()

    def wait_image_send(k):
        def one(r, carry):
            image_copy(k, lax.rem(me + r, N)).wait_send()
            return carry

        lax.fori_loop(1, N, one, 0)

    wait_image_send(0)

    @pl.when(split)
    def _():
        wait_image_send(1)

    def image_arrival(slot):
        return pltpu.make_async_remote_copy(
            src_ref=piece_in.at[slot],
            dst_ref=piece_in.at[slot],
            send_sem=image_recv.at[slot],
            recv_sem=image_recv.at[slot],
            device_id=(plane, up_w, tick),
            device_id_type=MESH,
        )

    def hand_out(slot):
        pltpu.make_async_copy(piece_in.at[slot], image_ref.at[slot], local.at[4]).start()

    def landed(slot):
        image_arrival(slot).wait_recv()
        hand_out(slot)

    def whole_images(r, carry):
        landed(lax.rem(mine + r, 8))
        return carry

    def split_images(r, carry):
        for k in range(2):
            for h in range(2):
                landed(8 + (2 * lax.rem(plane + r, 4) + k) * 2 + h)
        return carry

    lax.fori_loop(1, 8, whole_images, 0)
    lax.fori_loop(1, 4, split_images, 0)
    for k in range(2):
        landed(8 + (2 * plane + k) * 2 + 1 - half)

    @pl.when(split)
    def _():
        landed(mine)
        for k in range(2):
            hand_out(8 + (2 * plane + k) * 2 + half)

    @pl.when(whole)
    def _():
        hand_out(mine)
        for k in range(2):
            landed(8 + (2 * plane + k) * 2 + half)

    pltpu.make_async_copy(piece_in, image_ref, local.at[4]).wait()


def finish_kernel(signal_ref, piece_ref, signal_out, image_ref, held, pieces, image, sem):
    loads, stores = [], []
    for g in range(4):
        span = pl.ds(2 * g, 2)
        loads.append(
            (
                pltpu.make_async_copy(piece_ref.at[span], pieces.at[span], sem.at[0, g]),
                pltpu.make_async_copy(
                    piece_ref.at[pl.ds(8 + 4 * g, 4)], pieces.at[pl.ds(8 + 4 * g, 4)], sem.at[1, g]
                ),
                pltpu.make_async_copy(signal_ref.at[span], held.at[span], sem.at[2, g]),
            )
        )
        low, high = pl.ds(2 * g * TB, 2 * TB), pl.ds((8 + 2 * g) * TB, 2 * TB)
        stores.append(
            (
                pltpu.make_async_copy(image.at[:, low], image_ref.at[:, low], sem.at[3, g]),
                pltpu.make_async_copy(image.at[:, high], image_ref.at[:, high], sem.at[4, g]),
                pltpu.make_async_copy(held.at[span], signal_out.at[span], sem.at[5, g]),
            )
        )
    for load in loads:
        for copy in load:
            copy.start()
    for g in range(4):
        loads[g][0].wait()
        loads[g][1].wait()
        for j in (2 * g, 2 * g + 1):
            image[:, j * TB : (j + 1) * TB] = pieces[j].astype(F32)
            image[:, (8 + j) * TB : (9 + j) * TB] = pieces[8 + 2 * j].astype(F32) + pieces[
                9 + 2 * j
            ].astype(F32)
        stores[g][0].start()
        stores[g][1].start()
        loads[g][2].wait()
        stores[g][2].start()
    for store in stores:
        for copy in store:
            copy.wait()


def finish(signal, pieces):
    return pl.pallas_call(
        finish_kernel,
        out_shape=(
            jax.ShapeDtypeStruct((8, 32, 2048), BF16),
            jax.ShapeDtypeStruct((TB, 2048), F32),
        ),
        in_specs=[ANY, ANY],
        out_specs=(ANY, ANY),
        scratch_shapes=[
            pltpu.VMEM((8, 32, 2048), BF16),
            pltpu.VMEM((24, TB, TB), BF16),
            pltpu.VMEM((TB, 2048), F32),
            pltpu.SemaphoreType.DMA((6, 4)),
        ],
        compiler_params=pltpu.CompilerParams(vmem_limit_bytes=8 << 20),
        name="finish",
    )(signal, pieces)


def fused(raw, mask, taps, blocks, owners, geo):
    dma = pltpu.SemaphoreType.DMA
    return pl.pallas_call(
        kernel,
        out_shape=(
            jax.ShapeDtypeStruct((8, 32, 2048), BF16),
            jax.ShapeDtypeStruct((24, TB, TB), BF16),
        ),
        in_specs=[HBM, VMEM, VMEM, VMEM, VMEM, HBM],
        out_specs=(ANY, ANY),
        scratch_shapes=[
            pltpu.VMEM((256, 2048), BF16),
            pltpu.VMEM((24, 2 * TB), F32),
            pltpu.VMEM((8, TB), jnp.int32),
            pltpu.VMEM((2, 256, TB), BF16),
            pltpu.VMEM((2, 16, 2048), BF16),
            pltpu.VMEM((2, 256, TB), BF16),
            pltpu.VMEM((2, 16, 2048), BF16),
            pltpu.VMEM((4, 16, TB), BF16),
            pltpu.VMEM((256, TB), F32),
            pltpu.VMEM((288 * 18, TB), F32),
            pltpu.VMEM((3, 288, 16, TB), BF16),
            pltpu.VMEM((33 * TB, 2 * TB), BF16),
            pltpu.VMEM((ROWS, TB), F32),
            pltpu.VMEM((N, 8, 32, TB), BF16),
            pltpu.VMEM((65, 32, TB), BF16),
            pltpu.VMEM((65, 32, TB), BF16),
            pltpu.VMEM((N, 8, TB), F32),
            pltpu.VMEM((2, 8, 8, TB), F32),
            pltpu.VMEM((TB, 32, TB), BF16),
            pltpu.VMEM((2, 8, 2 * TB), jnp.int32),
            pltpu.SMEM((2, 8, 2 * TB), jnp.int32),
            pltpu.VMEM((2, BLOCKS + 1, TB, TB), F32),
            pltpu.VMEM((2, N, TB, TB), BF16),
            pltpu.VMEM((24, TB, TB), BF16),
            dma((8,)),
            dma((8,)),
            dma((N,)),
            dma((2, 8)),
            dma((N,)),
            dma((2, 8)),
            dma((2, N)),
            dma((24,)),
            dma((5,)),
        ],
        compiler_params=pltpu.CompilerParams(
            vmem_limit_bytes=LIMIT, collective_id=0, has_side_effects=True
        ),
        name="fused",
    )(raw, mask, taps, blocks, owners, geo)


def shards(raw, chan_mask, kernel_rows, geometry, roi_block, roi_owner):
    signal, pieces = fused(
        raw,
        chan_mask.reshape(1, 256),
        kernel_rows[0],
        roi_block.reshape(1, -1),
        roi_owner.reshape(1, -1),
        geometry,
    )
    signal, image = finish(signal, pieces)
    return (signal.reshape(256, 2048), image)


def solution(mesh):
    in_specs = (
        P(("plane", "wire"), "tick"),
        P(("plane", "wire")),
        P("plane", None, None),
        P(),
        P(("plane", "wire", "tick")),
        P(("plane", "wire", "tick")),
    )
    out_specs = (P(("plane", "wire"), "tick"), P(("plane", "wire"), "tick"))
    return jax.shard_map(shards, mesh=mesh, in_specs=in_specs, out_specs=out_specs, check_vma=False)
```

```python
import jax
import jax.numpy as jnp
from jax import lax
from jax.experimental import pallas as pl
from jax.experimental.pallas import tpu as pltpu
from jax.sharding import PartitionSpec as P

TB = 128
N = 16
CHUNK = 64
ROWS = CHUNK * 16
BLOCKS = 22
UNROLL = BLOCKS
LIMIT = 56 << 20
MESH = pl.DeviceIdType.MESH
VMEM = pl.BlockSpec(memory_space=pltpu.VMEM)
ANY = pl.BlockSpec(memory_space=pl.ANY)
HBM = pl.BlockSpec(memory_space=pltpu.HBM)
BF16 = jnp.bfloat16
F32 = jnp.float32


def row_of(ref, index, size):
    return ref.at[pl.ds(pl.multiple_of(index, size), size)]


def build_bands(taps_ref, band_ref):
    row = lax.broadcasted_iota(jnp.int32, (TB, TB), 0)
    col = lax.broadcasted_iota(jnp.int32, (TB, TB), 1)
    upper = col >= row
    zero = jnp.zeros((TB, TB), F32)

    def pair(m, carry):
        for p in range(2):
            taps = taps_ref[pl.ds(2 * m + p, 1), :]
            low, high = [
                pltpu.roll(
                    jnp.broadcast_to(taps[:, half * TB : (half + 1) * TB], (TB, TB)),
                    0,
                    1,
                    stride=1,
                    stride_axis=0,
                )
                for half in range(2)
            ]
            pieces = (
                jnp.where(upper, zero, high),
                jnp.where(upper, high, low),
                jnp.where(upper, low, zero),
            )
            for piece in range(3):
                start = pl.multiple_of((m * 3 + piece) * TB, TB)
                band_ref[pl.ds(start, TB), p * TB : (p + 1) * TB] = pieces[piece].astype(BF16)
        return carry

    lax.fori_loop(0, 11, pair, 0)


def kernel(
    raw_hbm,
    mask_ref,
    taps_ref,
    block_ref,
    owner_ref,
    geo_ref,
    signal_ref,
    image_ref,
    raw_ref,
    taps,
    roi_ref,
    edge_t,
    edge_w,
    halo_t,
    halo_w,
    halo_c,
    mask_col,
    tall,
    shifted,
    band,
    sums,
    sig,
    recv_0,
    recv_1,
    own_out,
    own_in,
    geo,
    plan_v,
    plan,
    runs,
    piece_out,
    piece_in,
    halo_send,
    halo_recv,
    own_send,
    own_recv,
    tile_send,
    tile_recv,
    image_send,
    image_recv,
    local,
):
    plane, wire, tick = lax.axis_index("plane"), lax.axis_index("wire"), lax.axis_index("tick")
    me = plane * 4 + wire
    recv = (recv_0, recv_1)
    half, inner = wire // 2, lax.rem(wire, 2)
    spot = plane * 2 + inner
    whole = jnp.logical_or(wire == 1, wire == 2)
    split = jnp.logical_not(whole)
    mine = plane * 2 + half
    up_t, down_t = lax.rem(tick + 1, 16), lax.rem(tick + 15, 16)
    up_w, down_w = lax.rem(wire + 1, 4), lax.rem(wire + 3, 4)

    def member(m):
        return (m // 4, lax.rem(m, 4), tick)

    barrier = pltpu.get_barrier_semaphore()

    def greet(r, carry):
        pl.semaphore_signal(barrier, inc=1, device_id=member(lax.rem(me + r, N)), device_id_type=MESH)
        return carry

    has = {"t+": tick < 15, "t-": tick > 0, "w+": wire < 3, "w-": wire > 0}

    def when_all(keys, action):
        test = has[keys[0]]
        for key in keys[1:]:
            test = jnp.logical_and(test, has[key])
        pl.when(test)(action)
        return test

    for t_key, t in (("t+", up_t), ("t-", down_t)):
        for w_keys, w in (((), wire), (("w+",), up_w), (("w-",), down_w)):

            def greet_side():
                pl.semaphore_signal(barrier, inc=1, device_id=(plane, w, t), device_id_type=MESH)

            when_all((t_key, *w_keys), greet_side)
    lax.fori_loop(1, N, greet, 0)

    raw_copy = pltpu.make_async_copy(raw_hbm, raw_ref, local.at[3])
    raw_copy.start()
    geo_copy = pltpu.make_async_copy(geo_ref, geo, local.at[0])
    taps[...] = jnp.zeros((24, 2 * TB), F32)
    taps[0:21, :] = taps_ref[...].astype(F32)
    roi_ref[...] = jnp.full((8, TB), -1, jnp.int32)
    roi_ref[0:1, 0:102] = block_ref[...]
    roi_ref[1:2, 0:102] = owner_ref[...]

    row = lax.broadcasted_iota(jnp.int32, (256, 256), 0)
    col = lax.broadcasted_iota(jnp.int32, (256, 256), 1)
    diag = jnp.where(row == col, mask_ref[...].astype(F32), 0.0).astype(BF16)
    mask_col[...] = jnp.dot(diag, jnp.ones((256, TB), BF16), preferred_element_type=F32)

    raw_copy.wait()
    geo_copy.start()
    for side, start in ((0, 0), (1, 15 * TB)):
        edge_t[side] = (raw_ref[:, start : start + TB].astype(F32) * mask_col[...]).astype(BF16)
    for side, start in ((0, 0), (1, 240)):
        for j in range(N):
            cols = slice(j * TB, (j + 1) * TB)
            edge_w[side, :, cols] = (
                raw_ref[start : start + 16, cols].astype(F32) * mask_col[start : start + 16, :]
            ).astype(BF16)

    ticks_near = (tick < 15).astype(jnp.int32) + (tick > 0).astype(jnp.int32)
    wires_near = 1 + (wire < 3).astype(jnp.int32) + (wire > 0).astype(jnp.int32)
    pl.semaphore_wait(barrier, 15 + ticks_near * wires_near)

    first, last = slice(0, TB), slice(15 * TB, 16 * TB)
    halo_copies = [
        pltpu.make_async_remote_copy(
            src_ref=src,
            dst_ref=dst,
            send_sem=halo_send.at[i],
            recv_sem=halo_recv.at[i],
            device_id=(plane, w, t),
            device_id_type=MESH,
        )
        for i, (src, dst, w, t) in enumerate(
            (
                (edge_t.at[1], halo_t.at[0], wire, up_t),
                (edge_t.at[0], halo_t.at[1], wire, down_t),
                (edge_w.at[1], halo_w.at[0], up_w, tick),
                (edge_w.at[0], halo_w.at[1], down_w, tick),
                (edge_w.at[1, :, last], halo_c.at[0], up_w, up_t),
                (edge_w.at[1, :, first], halo_c.at[1], up_w, down_t),
                (edge_w.at[0, :, last], halo_c.at[2], down_w, up_t),
                (edge_w.at[0, :, first], halo_c.at[3], down_w, down_t),
            )
        )
    ]
    outward = (("t+",), ("t-",), ("w+",), ("w-",), ("w+", "t+"), ("w+", "t-"), ("w-", "t+"), ("w-", "t-"))
    inward = (("t-",), ("t+",), ("w-",), ("w+",), ("w-", "t-"), ("w-", "t+"), ("w+", "t-"), ("w+", "t+"))
    landing = [halo_t.at[0], halo_t.at[1], halo_w.at[0], halo_w.at[1]] + [halo_c.at[i] for i in range(4)]
    for keys, copy in zip(outward, halo_copies):
        when_all(keys, copy.start)

    def take_halo(i):
        test = when_all(inward[i], halo_copies[i].wait_recv)

        @pl.when(jnp.logical_not(test))
        def _():
            landing[i][...] = jnp.zeros(landing[i].shape, BF16)

    def to_whole(r, turn, src, dst, send, receive):
        a = lax.rem(mine + r, 8)
        return pltpu.make_async_remote_copy(
            src_ref=src(a),
            dst_ref=dst(turn, spot),
            send_sem=send.at[a],
            recv_sem=receive.at[turn, spot],
            device_id=(a // 2, 1 + lax.rem(a, 2), tick),
            device_id_type=MESH,
        )

    def to_split(p, h, src, dst, send, receive):
        return pltpu.make_async_remote_copy(
            src_ref=src(8 + 2 * p + h),
            dst_ref=dst(h, spot),
            send_sem=send.at[8 + 2 * p + h],
            recv_sem=receive.at[h, spot],
            device_id=(p, 3 * half, tick),
            device_id_type=MESH,
        )

    def exchange(act, *refs):
        def across(i, carry):
            act(to_whole(2 * i + 1, 1, *refs))
            return carry

        def within(i, carry):
            act(to_whole(2 * i, 0, *refs))
            return carry

        def splits(r, carry):
            for h in range(2):
                act(to_split(lax.rem(plane + r, 4), h, *refs))
            return carry

        lax.fori_loop(0, 4, across, 0)
        lax.fori_loop(1, 4, within, 0)
        lax.fori_loop(1, 4, splits, 0)

        @pl.when(split)
        def _():
            act(to_whole(0, 0, *refs))

        @pl.when(whole)
        def _():
            for h in range(2):
                act(to_split(plane, h, *refs))

    def begin(copy):
        copy.start()

    def wait_send(copy):
        copy.wait_send()

    def side_of(turn):
        return jnp.where(whole, 1 - half, half) if turn else half

    def arrival(h, other, dst, receive):
        return pltpu.make_async_remote_copy(
            src_ref=dst(h, other),
            dst_ref=dst(h, other),
            send_sem=receive.at[h, other],
            recv_sem=receive.at[h, other],
            device_id=(other // 2, 2 * side_of(h) + lax.rem(other, 2), tick),
            device_id_type=MESH,
        )

    def wait_half(h, second, dst, receive):
        def one(r, carry):
            arrival(h, lax.rem(spot + r, 8), dst, receive).wait_recv()
            return carry

        lax.fori_loop(1, 8, one, 0)
        if second:

            @pl.when(whole)
            def _():
                arrival(h, spot, dst, receive).wait_recv()

    build_bands(taps, band)

    def spread(i, carry):
        wires = pl.ds(pl.multiple_of(i * 16, 16), 16)
        keep = mask_col[wires, :]
        for j in range(N):
            piece = raw_ref[wires, j * TB : (j + 1) * TB].astype(F32) * keep
            tall[pl.ds((i + 1) * 288 + j + 1, 16, stride=18), :] = piece
        return carry

    lax.fori_loop(0, 16, spread, 0)

    def window(i, carry):
        for u in range(8):
            slot = i * 8 + u
            for piece in range(3):
                shifted[piece, slot] = tall[pl.ds(slot * 18 + piece, 16), :].astype(BF16)
        return carry

    for i in (0, 1):
        take_halo(i)

    def spread_ticks(i, carry):
        wires = pl.ds(pl.multiple_of(i * 16, 16), 16)
        for side, j in ((0, 0), (1, 17)):
            tall[pl.ds((i + 1) * 288 + j, 16, stride=18), :] = halo_t[side, wires, :].astype(F32)
        return carry

    lax.fori_loop(0, 16, spread_ticks, 0)
    lax.fori_loop(CHUNK // 8, CHUNK // 8 + 4, window, 0)

    def run_chunk(base, size):
        lhs = jnp.concatenate(
            [
                shifted[piece, pl.ds(base + 6 + 2 * m, size + 1)].reshape((size + 1) * 16, TB)
                for m in range(11)
                for piece in range(3)
            ],
            axis=1,
        )
        both = jnp.dot(lhs, band[...], preferred_element_type=F32)
        sums[0 : size * 16] = both[: size * 16, :TB] + both[16:, TB:]
        tile = base // 32
        for j in range(N):
            for b in range(size // 16):
                sig[j, tile + b // 2, (b % 2) * 16 : (b % 2) * 16 + 16, :] = sums[
                    pl.ds(b * 256 + j, 16, stride=16), :
                ].astype(BF16)
        exchange(
            begin,
            lambda j: sig.at[j, pl.ds(tile, size // 32)],
            lambda h, i: recv[h].at[pl.ds(i * 8 + tile, size // 32)],
            tile_send,
            tile_recv,
        )

    own_refs = (lambda j: own_out.at[j], lambda h, i: own_in.at[h, i], own_send, own_recv)

    def share_owners():
        row = lax.broadcasted_iota(jnp.int32, (TB, TB), 0)
        hit = jnp.where(roi_ref[0:1, :] == lax.rem(row, 8) * 16 + row // 8, roi_ref[1:2, :] + 1, 0)
        table = jnp.dot(hit.astype(F32).astype(BF16), jnp.ones((TB, TB), BF16), preferred_element_type=F32)
        own_out[...] = table.reshape(N, 8, TB)

        exchange(begin, *own_refs)

        @pl.when(whole)
        def _():
            own_in[0, spot] = own_out[mine]

        @pl.when(split)
        def _():
            for h in range(2):
                own_in[h, spot] = own_out[8 + 2 * plane + h]

    def take_wires():
        for i in range(2, 8):
            take_halo(i)
        for side, base in ((0, 0), (1, 272 * 18)):
            for j in range(N):
                tall[pl.ds(base + j + 1, 16, stride=18), :] = halo_w[side, :, j * TB : (j + 1) * TB].astype(F32)
            for t, j in ((0, 0), (1, 17)):
                tall[pl.ds(base + j, 16, stride=18), :] = halo_c[side * 2 + t].astype(F32)

    chunks = 256 // CHUNK

    def step(n, carry):
        c = lax.rem(n + 1, chunks)
        pl.when(n == chunks - 2)(take_wires)
        slots = jnp.where(c == 0, 0, (c * CHUNK + 32) // 8)
        lax.fori_loop(slots, slots + CHUNK // 8, window, 0)
        run_chunk(c * CHUNK, CHUNK)
        pl.when(n == 0)(share_owners)
        return carry

    lax.fori_loop(0, chunks, step, 0)

    def store_signal(j, carry):
        pltpu.make_async_copy(
            sig.at[j], signal_ref.at[:, :, pl.ds(pl.multiple_of(j * TB, TB), TB)], local.at[1]
        ).start()
        return carry

    lax.fori_loop(0, N, store_signal, 0)

    @pl.when(whole)
    def _():
        recv[0][pl.ds(spot * 8, 8)] = sig[mine]

    @pl.when(split)
    def _():
        for h in range(2):
            recv[h][pl.ds(spot * 8, 8)] = sig[8 + 2 * plane + h]

    own_dst, tile_dst = own_refs[1], lambda h, i: recv[h].at[pl.ds(i * 8, 8)]
    wait_half(0, False, own_dst, own_recv)
    wait_half(1, True, own_dst, own_recv)

    tile = lax.broadcasted_iota(jnp.int32, (64, TB), 0)
    lane = lax.broadcasted_iota(jnp.int32, (64, TB), 1)
    place = lax.broadcasted_iota(jnp.int32, (64, 2 * TB), 1).astype(F32)
    before = (lax.broadcasted_iota(jnp.int32, (64, 64), 1) < lax.broadcasted_iota(jnp.int32, (64, 64), 0)).astype(
        F32
    )
    lower = (lax.broadcasted_iota(jnp.int32, (TB, TB), 0) < lax.broadcasted_iota(jnp.int32, (TB, TB), 1)).astype(
        F32
    )
    for h in range(2):
        side = side_of(h)
        georow = ((tile // 16) * 4 + 2 * side + lax.rem(tile // 8, 2)) * 8 + lax.rem(tile, 8)
        wanted = own_in[h].reshape(64, TB)
        member_of = jnp.where(wanted == (lane + 1).astype(F32), 1.0, 0.0)
        rank = jnp.dot(before.astype(BF16), member_of.astype(BF16), preferred_element_type=F32)
        count = jnp.sum(member_of, axis=0, keepdims=True)
        blocks = jnp.floor((count + 7.0) * 0.125)
        opening = jnp.dot(
            jnp.broadcast_to(blocks, (8, TB)).astype(BF16), lower.astype(BF16), preferred_element_type=F32
        )[0:1, :]
        found = jnp.sum(member_of, axis=1, keepdims=True)
        spot_of = jnp.sum(member_of * (opening * 8.0 + rank), axis=1, keepdims=True) - (1.0 - found)
        rank_of = jnp.sum(member_of * rank, axis=1, keepdims=True)
        here = jnp.where(spot_of == place, 1.0, 0.0)
        tile_f, geo_f = tile[:, 0:1].astype(F32), georow[:, 0:1].astype(F32)
        plan_v[h, 0:1, :] = (64.0 + jnp.sum(here * (tile_f - 64.0), axis=0, keepdims=True)).astype(jnp.int32)
        plan_v[h, 1:2, :] = jnp.sum(here * geo_f, axis=0, keepdims=True).astype(jnp.int32)
        again = jnp.where(spot_of == place * 8.0, 1.0, 0.0) * jnp.where(rank_of > 0.0, 1.0, 0.0)
        plan_v[h, 2:3, :] = jnp.sum(again, axis=0, keepdims=True).astype(jnp.int32)
        closing = jnp.where(count > 0.0, opening + blocks - 1.0, float(BLOCKS))
        plan_v[h, 3:4, 0:TB] = closing.astype(jnp.int32)
        plan_v[h, 3:4, TB : 2 * TB] = closing.astype(jnp.int32)
        plan_v[h, 4:8, :] = jnp.zeros((4, 2 * TB), jnp.int32)
        recv[h][64] = jnp.zeros((32, TB), BF16)
        runs[h, BLOCKS] = jnp.zeros((TB, TB), F32)
    plan_copy = pltpu.make_async_copy(plan_v, plan, local.at[2])
    plan_copy.start()
    geo_copy.wait()
    plan_copy.wait()

    def image_slot(p, w, h, k):
        outer = jnp.logical_or(w == 0, w == 3)
        return jnp.where(outer, 8 + (2 * p + k) * 2 + h, 2 * p + h)

    def image_copy(k, o):
        slot = image_slot(plane, wire, half, k)
        return pltpu.make_async_remote_copy(
            src_ref=piece_out.at[k, o],
            dst_ref=piece_in.at[slot],
            send_sem=image_send.at[k, o],
            recv_sem=image_recv.at[slot],
            device_id=member(o),
            device_id_type=MESH,
        )

    both_halves = jnp.where(whole, 1.0, 0.0)
    for h in range(2):
        k = 0 if h == 0 else jnp.where(whole, 0, 1)
        wait_half(h, h == 1, tile_dst, tile_recv)

        def block(b, run):
            lhs = jnp.concatenate([geo[jnp.clip(plan[h, 1, b * 8 + i], 0, TB - 1)] for i in range(8)], axis=0)
            rhs = jnp.concatenate([recv[h][jnp.clip(plan[h, 0, b * 8 + i], 0, 64)] for i in range(8)], axis=0)
            part = lax.dot_general(lhs, rhs, (((0,), (0,)), ((), ())), preferred_element_type=F32)
            run = run * plan[h, 2, b].astype(F32) + part
            runs[h, b] = run
            return run

        lax.fori_loop(0, BLOCKS, block, jnp.zeros((TB, TB), F32), unroll=UNROLL)

        for i in range(N):
            o = lax.rem(plane + 1 + i // 2, 4) * 4
            if i < 8:
                o += 2 * (1 - half) + i % 2
            else:
                o += 2 * half + lax.rem(inner + 1 + i, 2)

            def send_piece():
                now = runs[h, jnp.clip(plan[h, 3, o], 0, BLOCKS)]
                if h == 1:
                    now = now + runs[0, jnp.clip(plan[0, 3, o], 0, BLOCKS)] * both_halves
                piece_out[k, o] = now.astype(BF16)
                if i < N - 1:
                    image_copy(k, o).start()
                else:
                    piece_in[image_slot(plane, wire, half, k)] = piece_out[k, o]

            if h == 0:
                pl.when(split)(send_piece)
            else:
                send_piece()

    for keys, copy in zip(outward, halo_copies):
        when_all(keys, copy.wait_send)
    exchange(wait_send, *own_refs)
    exchange(wait_send, lambda j: sig.at[j], tile_dst, tile_send, tile_recv)
    pltpu.make_async_copy(signal_ref, signal_ref, local.at[1]).wait()

    def wait_image_send(k):
        def one(r, carry):
            image_copy(k, lax.rem(me + r, N)).wait_send()
            return carry

        lax.fori_loop(1, N, one, 0)

    wait_image_send(0)

    @pl.when(split)
    def _():
        wait_image_send(1)

    def image_arrival(slot):
        return pltpu.make_async_remote_copy(
            src_ref=piece_in.at[slot],
            dst_ref=piece_in.at[slot],
            send_sem=image_recv.at[slot],
            recv_sem=image_recv.at[slot],
            device_id=(plane, up_w, tick),
            device_id_type=MESH,
        )

    def hand_out(slot):
        pltpu.make_async_copy(piece_in.at[slot], image_ref.at[slot], local.at[4]).start()

    def landed(slot):
        image_arrival(slot).wait_recv()
        hand_out(slot)

    def whole_images(r, carry):
        landed(lax.rem(mine + r, 8))
        return carry

    def split_images(r, carry):
        for k in range(2):
            for h in range(2):
                landed(8 + (2 * lax.rem(plane + r, 4) + k) * 2 + h)
        return carry

    lax.fori_loop(1, 8, whole_images, 0)
    lax.fori_loop(1, 4, split_images, 0)
    for k in range(2):
        landed(8 + (2 * plane + k) * 2 + 1 - half)

    @pl.when(split)
    def _():
        landed(mine)
        for k in range(2):
            hand_out(8 + (2 * plane + k) * 2 + half)

    @pl.when(whole)
    def _():
        hand_out(mine)
        for k in range(2):
            landed(8 + (2 * plane + k) * 2 + half)

    pltpu.make_async_copy(piece_in, image_ref, local.at[4]).wait()


def finish_kernel(signal_ref, piece_ref, signal_out, image_ref, held, pieces, image, sem):
    loads, stores = [], []
    for g in range(4):
        span = pl.ds(2 * g, 2)
        loads.append(
            (
                pltpu.make_async_copy(piece_ref.at[span], pieces.at[span], sem.at[0, g]),
                pltpu.make_async_copy(
                    piece_ref.at[pl.ds(8 + 4 * g, 4)], pieces.at[pl.ds(8 + 4 * g, 4)], sem.at[1, g]
                ),
                pltpu.make_async_copy(signal_ref.at[span], held.at[span], sem.at[2, g]),
            )
        )
        low, high = pl.ds(2 * g * TB, 2 * TB), pl.ds((8 + 2 * g) * TB, 2 * TB)
        stores.append(
            (
                pltpu.make_async_copy(image.at[:, low], image_ref.at[:, low], sem.at[3, g]),
                pltpu.make_async_copy(image.at[:, high], image_ref.at[:, high], sem.at[4, g]),
                pltpu.make_async_copy(held.at[span], signal_out.at[span], sem.at[5, g]),
            )
        )
    for load in loads:
        for copy in load:
            copy.start()
    for g in range(4):
        loads[g][0].wait()
        loads[g][1].wait()
        for j in (2 * g, 2 * g + 1):
            image[:, j * TB : (j + 1) * TB] = pieces[j].astype(F32)
            image[:, (8 + j) * TB : (9 + j) * TB] = pieces[8 + 2 * j].astype(F32) + pieces[
                9 + 2 * j
            ].astype(F32)
        stores[g][0].start()
        stores[g][1].start()
        loads[g][2].wait()
        stores[g][2].start()
    for store in stores:
        for copy in store:
            copy.wait()


def finish(signal, pieces):
    return pl.pallas_call(
        finish_kernel,
        out_shape=(
            jax.ShapeDtypeStruct((8, 32, 2048), BF16),
            jax.ShapeDtypeStruct((TB, 2048), F32),
        ),
        in_specs=[ANY, ANY],
        out_specs=(ANY, ANY),
        scratch_shapes=[
            pltpu.VMEM((8, 32, 2048), BF16),
            pltpu.VMEM((24, TB, TB), BF16),
            pltpu.VMEM((TB, 2048), F32),
            pltpu.SemaphoreType.DMA((6, 4)),
        ],
        compiler_params=pltpu.CompilerParams(vmem_limit_bytes=LIMIT),
        name="finish",
    )(signal, pieces)


def fused(raw, mask, taps, blocks, owners, geo):
    dma = pltpu.SemaphoreType.DMA
    return pl.pallas_call(
        kernel,
        out_shape=(
            jax.ShapeDtypeStruct((8, 32, 2048), BF16),
            jax.ShapeDtypeStruct((24, TB, TB), BF16),
        ),
        in_specs=[HBM, VMEM, VMEM, VMEM, VMEM, HBM],
        out_specs=(ANY, ANY),
        scratch_shapes=[
            pltpu.VMEM((256, 2048), BF16),
            pltpu.VMEM((24, 2 * TB), F32),
            pltpu.VMEM((8, TB), jnp.int32),
            pltpu.VMEM((2, 256, TB), BF16),
            pltpu.VMEM((2, 16, 2048), BF16),
            pltpu.VMEM((2, 256, TB), BF16),
            pltpu.VMEM((2, 16, 2048), BF16),
            pltpu.VMEM((4, 16, TB), BF16),
            pltpu.VMEM((256, TB), F32),
            pltpu.VMEM((288 * 18, TB), F32),
            pltpu.VMEM((3, 288, 16, TB), BF16),
            pltpu.VMEM((33 * TB, 2 * TB), BF16),
            pltpu.VMEM((ROWS, TB), F32),
            pltpu.VMEM((N, 8, 32, TB), BF16),
            pltpu.VMEM((65, 32, TB), BF16),
            pltpu.VMEM((65, 32, TB), BF16),
            pltpu.VMEM((N, 8, TB), F32),
            pltpu.VMEM((2, 8, 8, TB), F32),
            pltpu.VMEM((TB, 32, TB), BF16),
            pltpu.VMEM((2, 8, 2 * TB), jnp.int32),
            pltpu.SMEM((2, 8, 2 * TB), jnp.int32),
            pltpu.VMEM((2, BLOCKS + 1, TB, TB), F32),
            pltpu.VMEM((2, N, TB, TB), BF16),
            pltpu.VMEM((24, TB, TB), BF16),
            dma((8,)),
            dma((8,)),
            dma((N,)),
            dma((2, 8)),
            dma((N,)),
            dma((2, 8)),
            dma((2, N)),
            dma((24,)),
            dma((5,)),
        ],
        compiler_params=pltpu.CompilerParams(
            vmem_limit_bytes=LIMIT, collective_id=0, has_side_effects=True
        ),
        name="fused",
    )(raw, mask, taps, blocks, owners, geo)


def shards(raw, chan_mask, kernel_rows, geometry, roi_block, roi_owner):
    signal, pieces = fused(
        raw,
        chan_mask.reshape(1, 256),
        kernel_rows[0],
        roi_block.reshape(1, -1),
        roi_owner.reshape(1, -1),
        geometry,
    )
    signal, image = finish(signal, pieces)
    return (signal.reshape(256, 2048), image)


def solution(mesh):
    in_specs = (
        P(("plane", "wire"), "tick"),
        P(("plane", "wire")),
        P("plane", None, None),
        P(),
        P(("plane", "wire", "tick")),
        P(("plane", "wire", "tick")),
    )
    out_specs = (P(("plane", "wire"), "tick"), P(("plane", "wire"), "tick"))
    return jax.shard_map(shards, mesh=mesh, in_specs=in_specs, out_specs=out_specs, check_vma=False)
```

```python
import jax
import jax.numpy as jnp
from jax import lax
from jax.experimental import pallas as pl
from jax.experimental.pallas import tpu as pltpu
from jax.sharding import PartitionSpec as P

TB = 128
N = 16
CHUNK = 64
ROWS = CHUNK * 16
EARLY = 4
BLOCKS = 22
UNROLL = BLOCKS
LIMIT = 56 << 20
MESH = pl.DeviceIdType.MESH
VMEM = pl.BlockSpec(memory_space=pltpu.VMEM)
ANY = pl.BlockSpec(memory_space=pl.ANY)
HBM = pl.BlockSpec(memory_space=pltpu.HBM)
BF16 = jnp.bfloat16
F32 = jnp.float32


def row_of(ref, index, size):
    return ref.at[pl.ds(pl.multiple_of(index, size), size)]


def build_bands(taps_ref, band_ref, first, last):
    row = lax.broadcasted_iota(jnp.int32, (TB, TB), 0)
    col = lax.broadcasted_iota(jnp.int32, (TB, TB), 1)
    upper = col >= row
    zero = jnp.zeros((TB, TB), F32)

    def pair(m, carry):
        for p in range(2):
            taps = taps_ref[pl.ds(2 * m + p, 1), :]
            low, high = [
                pltpu.roll(
                    jnp.broadcast_to(taps[:, half * TB : (half + 1) * TB], (TB, TB)),
                    0,
                    1,
                    stride=1,
                    stride_axis=0,
                )
                for half in range(2)
            ]
            pieces = (
                jnp.where(upper, zero, high),
                jnp.where(upper, high, low),
                jnp.where(upper, low, zero),
            )
            for piece in range(3):
                start = pl.multiple_of((m * 3 + piece) * TB, TB)
                band_ref[pl.ds(start, TB), p * TB : (p + 1) * TB] = pieces[piece].astype(BF16)
        return carry

    lax.fori_loop(first, last, pair, 0)


def kernel(
    raw_hbm,
    mask_ref,
    taps_ref,
    block_ref,
    owner_ref,
    geo_ref,
    signal_ref,
    image_ref,
    raw_ref,
    taps,
    roi_ref,
    edge_t,
    edge_w,
    halo_t,
    halo_w,
    halo_c,
    mask_col,
    tall,
    shifted,
    band,
    sums,
    sig,
    recv_0,
    recv_1,
    own_out,
    own_in,
    geo,
    plan_v,
    plan,
    runs,
    piece_out,
    piece_in,
    halo_send,
    halo_recv,
    own_send,
    own_recv,
    tile_send,
    tile_recv,
    image_send,
    image_recv,
    local,
):
    plane, wire, tick = lax.axis_index("plane"), lax.axis_index("wire"), lax.axis_index("tick")
    me = plane * 4 + wire
    recv = (recv_0, recv_1)
    half, inner = wire // 2, lax.rem(wire, 2)
    spot = plane * 2 + inner
    whole = jnp.logical_or(wire == 1, wire == 2)
    split = jnp.logical_not(whole)
    mine = plane * 2 + half
    up_t, down_t = lax.rem(tick + 1, 16), lax.rem(tick + 15, 16)
    up_w, down_w = lax.rem(wire + 1, 4), lax.rem(wire + 3, 4)

    def member(m):
        return (m // 4, lax.rem(m, 4), tick)

    raw_copy = pltpu.make_async_copy(raw_hbm, raw_ref, local.at[3])
    raw_copy.start()
    barrier = pltpu.get_barrier_semaphore()

    def greet(r, carry):
        pl.semaphore_signal(barrier, inc=1, device_id=member(lax.rem(me + r, N)), device_id_type=MESH)
        return carry

    has = {"t+": tick < 15, "t-": tick > 0, "w+": wire < 3, "w-": wire > 0}

    def when_all(keys, action):
        test = has[keys[0]]
        for key in keys[1:]:
            test = jnp.logical_and(test, has[key])
        pl.when(test)(action)
        return test

    for t_key, t in (("t+", up_t), ("t-", down_t)):
        for w_keys, w in (((), wire), (("w+",), up_w), (("w-",), down_w)):

            def greet_side():
                pl.semaphore_signal(barrier, inc=1, device_id=(plane, w, t), device_id_type=MESH)

            when_all((t_key, *w_keys), greet_side)
    lax.fori_loop(1, N, greet, 0)

    geo_copy = pltpu.make_async_copy(geo_ref, geo, local.at[0])
    taps[...] = jnp.zeros((24, 2 * TB), F32)
    taps[0:21, :] = taps_ref[...].astype(F32)
    roi_ref[...] = jnp.full((8, TB), -1, jnp.int32)
    roi_ref[0:1, 0:102] = block_ref[...]
    roi_ref[1:2, 0:102] = owner_ref[...]

    row = lax.broadcasted_iota(jnp.int32, (256, 256), 0)
    col = lax.broadcasted_iota(jnp.int32, (256, 256), 1)
    diag = jnp.where(row == col, mask_ref[...].astype(F32), 0.0).astype(BF16)
    mask_col[...] = jnp.dot(diag, jnp.ones((256, TB), BF16), preferred_element_type=F32)

    build_bands(taps, band, 0, EARLY)
    raw_copy.wait()
    geo_copy.start()
    for side, start in ((0, 0), (1, 15 * TB)):
        edge_t[side] = (raw_ref[:, start : start + TB].astype(F32) * mask_col[...]).astype(BF16)
    for side, start in ((0, 0), (1, 240)):
        for j in range(N):
            cols = slice(j * TB, (j + 1) * TB)
            edge_w[side, :, cols] = (
                raw_ref[start : start + 16, cols].astype(F32) * mask_col[start : start + 16, :]
            ).astype(BF16)

    ticks_near = (tick < 15).astype(jnp.int32) + (tick > 0).astype(jnp.int32)
    wires_near = 1 + (wire < 3).astype(jnp.int32) + (wire > 0).astype(jnp.int32)
    pl.semaphore_wait(barrier, 15 + ticks_near * wires_near)

    first, last = slice(0, TB), slice(15 * TB, 16 * TB)
    halo_copies = [
        pltpu.make_async_remote_copy(
            src_ref=src,
            dst_ref=dst,
            send_sem=halo_send.at[i],
            recv_sem=halo_recv.at[i],
            device_id=(plane, w, t),
            device_id_type=MESH,
        )
        for i, (src, dst, w, t) in enumerate(
            (
                (edge_t.at[1], halo_t.at[0], wire, up_t),
                (edge_t.at[0], halo_t.at[1], wire, down_t),
                (edge_w.at[1], halo_w.at[0], up_w, tick),
                (edge_w.at[0], halo_w.at[1], down_w, tick),
                (edge_w.at[1, :, last], halo_c.at[0], up_w, up_t),
                (edge_w.at[1, :, first], halo_c.at[1], up_w, down_t),
                (edge_w.at[0, :, last], halo_c.at[2], down_w, up_t),
                (edge_w.at[0, :, first], halo_c.at[3], down_w, down_t),
            )
        )
    ]
    outward = (("t+",), ("t-",), ("w+",), ("w-",), ("w+", "t+"), ("w+", "t-"), ("w-", "t+"), ("w-", "t-"))
    inward = (("t-",), ("t+",), ("w-",), ("w+",), ("w-", "t-"), ("w-", "t+"), ("w+", "t-"), ("w+", "t+"))
    landing = [halo_t.at[0], halo_t.at[1], halo_w.at[0], halo_w.at[1]] + [halo_c.at[i] for i in range(4)]
    for keys, copy in zip(outward, halo_copies):
        when_all(keys, copy.start)

    def take_halo(i):
        test = when_all(inward[i], halo_copies[i].wait_recv)

        @pl.when(jnp.logical_not(test))
        def _():
            landing[i][...] = jnp.zeros(landing[i].shape, BF16)

    def to_whole(r, turn, src, dst, send, receive):
        a = lax.rem(mine + r, 8)
        return pltpu.make_async_remote_copy(
            src_ref=src(a),
            dst_ref=dst(turn, spot),
            send_sem=send.at[a],
            recv_sem=receive.at[turn, spot],
            device_id=(a // 2, 1 + lax.rem(a, 2), tick),
            device_id_type=MESH,
        )

    def to_split(p, h, src, dst, send, receive):
        return pltpu.make_async_remote_copy(
            src_ref=src(8 + 2 * p + h),
            dst_ref=dst(h, spot),
            send_sem=send.at[8 + 2 * p + h],
            recv_sem=receive.at[h, spot],
            device_id=(p, 3 * half, tick),
            device_id_type=MESH,
        )

    def exchange(act, *refs):
        def across(i, carry):
            act(to_whole(2 * i + 1, 1, *refs))
            return carry

        def within(i, carry):
            act(to_whole(2 * i, 0, *refs))
            return carry

        def splits(r, carry):
            for h in range(2):
                act(to_split(lax.rem(plane + r, 4), h, *refs))
            return carry

        lax.fori_loop(0, 4, across, 0)
        lax.fori_loop(1, 4, within, 0)
        lax.fori_loop(1, 4, splits, 0)

        @pl.when(split)
        def _():
            act(to_whole(0, 0, *refs))

        @pl.when(whole)
        def _():
            for h in range(2):
                act(to_split(plane, h, *refs))

    def begin(copy):
        copy.start()

    def wait_send(copy):
        copy.wait_send()

    def side_of(turn):
        return jnp.where(whole, 1 - half, half) if turn else half

    def arrival(h, other, dst, receive):
        return pltpu.make_async_remote_copy(
            src_ref=dst(h, other),
            dst_ref=dst(h, other),
            send_sem=receive.at[h, other],
            recv_sem=receive.at[h, other],
            device_id=(other // 2, 2 * side_of(h) + lax.rem(other, 2), tick),
            device_id_type=MESH,
        )

    def wait_half(h, second, dst, receive):
        def one(r, carry):
            arrival(h, lax.rem(spot + r, 8), dst, receive).wait_recv()
            return carry

        lax.fori_loop(1, 8, one, 0)
        if second:

            @pl.when(whole)
            def _():
                arrival(h, spot, dst, receive).wait_recv()

    build_bands(taps, band, EARLY, 11)

    def spread(i, carry):
        wires = pl.ds(pl.multiple_of(i * 16, 16), 16)
        keep = mask_col[wires, :]
        for j in range(N):
            piece = raw_ref[wires, j * TB : (j + 1) * TB].astype(F32) * keep
            tall[pl.ds((i + 1) * 288 + j + 1, 16, stride=18), :] = piece
        return carry

    lax.fori_loop(0, 16, spread, 0)

    def window(i, carry):
        for u in range(8):
            slot = i * 8 + u
            for piece in range(3):
                shifted[piece, slot] = tall[pl.ds(slot * 18 + piece, 16), :].astype(BF16)
        return carry

    for i in (0, 1):
        take_halo(i)

    def spread_ticks(i, carry):
        wires = pl.ds(pl.multiple_of(i * 16, 16), 16)
        for side, j in ((0, 0), (1, 17)):
            tall[pl.ds((i + 1) * 288 + j, 16, stride=18), :] = halo_t[side, wires, :].astype(F32)
        return carry

    lax.fori_loop(0, 16, spread_ticks, 0)
    lax.fori_loop(CHUNK // 8, CHUNK // 8 + 4, window, 0)

    def run_chunk(base, size):
        lhs = jnp.concatenate(
            [
                shifted[piece, pl.ds(base + 6 + 2 * m, size + 1)].reshape((size + 1) * 16, TB)
                for m in range(11)
                for piece in range(3)
            ],
            axis=1,
        )
        both = jnp.dot(lhs, band[...], preferred_element_type=F32)
        sums[0 : size * 16] = both[: size * 16, :TB] + both[16:, TB:]
        tile = base // 32
        for j in range(N):
            for b in range(size // 16):
                sig[j, tile + b // 2, (b % 2) * 16 : (b % 2) * 16 + 16, :] = sums[
                    pl.ds(b * 256 + j, 16, stride=16), :
                ].astype(BF16)
        exchange(
            begin,
            lambda j: sig.at[j, pl.ds(tile, size // 32)],
            lambda h, i: recv[h].at[pl.ds(i * 8 + tile, size // 32)],
            tile_send,
            tile_recv,
        )

    own_refs = (lambda j: own_out.at[j], lambda h, i: own_in.at[h, i], own_send, own_recv)

    def share_owners():
        row = lax.broadcasted_iota(jnp.int32, (TB, TB), 0)
        hit = jnp.where(roi_ref[0:1, :] == lax.rem(row, 8) * 16 + row // 8, roi_ref[1:2, :] + 1, 0)
        table = jnp.dot(hit.astype(F32).astype(BF16), jnp.ones((TB, TB), BF16), preferred_element_type=F32)
        own_out[...] = table.reshape(N, 8, TB)

        exchange(begin, *own_refs)

        @pl.when(whole)
        def _():
            own_in[0, spot] = own_out[mine]

        @pl.when(split)
        def _():
            for h in range(2):
                own_in[h, spot] = own_out[8 + 2 * plane + h]

    def take_wires():
        for i in range(2, 8):
            take_halo(i)
        for side, base in ((0, 0), (1, 272 * 18)):
            for j in range(N):
                tall[pl.ds(base + j + 1, 16, stride=18), :] = halo_w[side, :, j * TB : (j + 1) * TB].astype(F32)
            for t, j in ((0, 0), (1, 17)):
                tall[pl.ds(base + j, 16, stride=18), :] = halo_c[side * 2 + t].astype(F32)

    chunks = 256 // CHUNK

    def step(n, carry):
        c = lax.rem(n + 1, chunks)
        pl.when(n == chunks - 2)(take_wires)
        slots = jnp.where(c == 0, 0, (c * CHUNK + 32) // 8)
        lax.fori_loop(slots, slots + CHUNK // 8, window, 0)
        run_chunk(c * CHUNK, CHUNK)
        pl.when(n == 0)(share_owners)
        return carry

    lax.fori_loop(0, chunks, step, 0)

    def store_signal(j, carry):
        pltpu.make_async_copy(
            sig.at[j], signal_ref.at[:, :, pl.ds(pl.multiple_of(j * TB, TB), TB)], local.at[1]
        ).start()
        return carry

    lax.fori_loop(0, N, store_signal, 0)

    @pl.when(whole)
    def _():
        recv[0][pl.ds(spot * 8, 8)] = sig[mine]

    @pl.when(split)
    def _():
        for h in range(2):
            recv[h][pl.ds(spot * 8, 8)] = sig[8 + 2 * plane + h]

    own_dst, tile_dst = own_refs[1], lambda h, i: recv[h].at[pl.ds(i * 8, 8)]
    wait_half(0, False, own_dst, own_recv)
    wait_half(1, True, own_dst, own_recv)

    tile = lax.broadcasted_iota(jnp.int32, (64, TB), 0)
    lane = lax.broadcasted_iota(jnp.int32, (64, TB), 1)
    place = lax.broadcasted_iota(jnp.int32, (64, 2 * TB), 1).astype(F32)
    before = (lax.broadcasted_iota(jnp.int32, (64, 64), 1) < lax.broadcasted_iota(jnp.int32, (64, 64), 0)).astype(
        F32
    )
    lower = (lax.broadcasted_iota(jnp.int32, (TB, TB), 0) < lax.broadcasted_iota(jnp.int32, (TB, TB), 1)).astype(
        F32
    )
    for h in range(2):
        side = side_of(h)
        georow = ((tile // 16) * 4 + 2 * side + lax.rem(tile // 8, 2)) * 8 + lax.rem(tile, 8)
        wanted = own_in[h].reshape(64, TB)
        member_of = jnp.where(wanted == (lane + 1).astype(F32), 1.0, 0.0)
        rank = jnp.dot(before.astype(BF16), member_of.astype(BF16), preferred_element_type=F32)
        count = jnp.sum(member_of, axis=0, keepdims=True)
        blocks = jnp.floor((count + 7.0) * 0.125)
        opening = jnp.dot(
            jnp.broadcast_to(blocks, (8, TB)).astype(BF16), lower.astype(BF16), preferred_element_type=F32
        )[0:1, :]
        found = jnp.sum(member_of, axis=1, keepdims=True)
        spot_of = jnp.sum(member_of * (opening * 8.0 + rank), axis=1, keepdims=True) - (1.0 - found)
        rank_of = jnp.sum(member_of * rank, axis=1, keepdims=True)
        here = jnp.where(spot_of == place, 1.0, 0.0)
        tile_f, geo_f = tile[:, 0:1].astype(F32), georow[:, 0:1].astype(F32)
        plan_v[h, 0:1, :] = (64.0 + jnp.sum(here * (tile_f - 64.0), axis=0, keepdims=True)).astype(jnp.int32)
        plan_v[h, 1:2, :] = jnp.sum(here * geo_f, axis=0, keepdims=True).astype(jnp.int32)
        again = jnp.where(spot_of == place * 8.0, 1.0, 0.0) * jnp.where(rank_of > 0.0, 1.0, 0.0)
        plan_v[h, 2:3, :] = jnp.sum(again, axis=0, keepdims=True).astype(jnp.int32)
        closing = jnp.where(count > 0.0, opening + blocks - 1.0, float(BLOCKS))
        plan_v[h, 3:4, 0:TB] = closing.astype(jnp.int32)
        plan_v[h, 3:4, TB : 2 * TB] = closing.astype(jnp.int32)
        plan_v[h, 4:8, :] = jnp.zeros((4, 2 * TB), jnp.int32)
        recv[h][64] = jnp.zeros((32, TB), BF16)
        runs[h, BLOCKS] = jnp.zeros((TB, TB), F32)
    plan_copy = pltpu.make_async_copy(plan_v, plan, local.at[2])
    plan_copy.start()
    geo_copy.wait()
    plan_copy.wait()

    def image_slot(p, w, h, k):
        outer = jnp.logical_or(w == 0, w == 3)
        return jnp.where(outer, 8 + (2 * p + k) * 2 + h, 2 * p + h)

    def image_copy(k, o):
        slot = image_slot(plane, wire, half, k)
        return pltpu.make_async_remote_copy(
            src_ref=piece_out.at[k, o],
            dst_ref=piece_in.at[slot],
            send_sem=image_send.at[k, o],
            recv_sem=image_recv.at[slot],
            device_id=member(o),
            device_id_type=MESH,
        )

    both_halves = jnp.where(whole, 1.0, 0.0)
    for h in range(2):
        k = 0 if h == 0 else jnp.where(whole, 0, 1)
        wait_half(h, h == 1, tile_dst, tile_recv)

        def block(b, run):
            lhs = jnp.concatenate([geo[jnp.clip(plan[h, 1, b * 8 + i], 0, TB - 1)] for i in range(8)], axis=0)
            rhs = jnp.concatenate([recv[h][jnp.clip(plan[h, 0, b * 8 + i], 0, 64)] for i in range(8)], axis=0)
            part = lax.dot_general(lhs, rhs, (((0,), (0,)), ((), ())), preferred_element_type=F32)
            run = run * plan[h, 2, b].astype(F32) + part
            runs[h, b] = run
            return run

        lax.fori_loop(0, BLOCKS, block, jnp.zeros((TB, TB), F32), unroll=UNROLL)

        for i in range(N):
            o = lax.rem(plane + 1 + i // 2, 4) * 4
            if i < 8:
                o += 2 * (1 - half) + i % 2
            else:
                o += 2 * half + lax.rem(inner + 1 + i, 2)

            def send_piece():
                now = runs[h, jnp.clip(plan[h, 3, o], 0, BLOCKS)]
                if h == 1:
                    now = now + runs[0, jnp.clip(plan[0, 3, o], 0, BLOCKS)] * both_halves
                piece_out[k, o] = now.astype(BF16)
                if i < N - 1:
                    image_copy(k, o).start()
                else:
                    piece_in[image_slot(plane, wire, half, k)] = piece_out[k, o]

            if h == 0:
                pl.when(split)(send_piece)
            else:
                send_piece()

    for keys, copy in zip(outward, halo_copies):
        when_all(keys, copy.wait_send)
    exchange(wait_send, *own_refs)
    exchange(wait_send, lambda j: sig.at[j], tile_dst, tile_send, tile_recv)
    pltpu.make_async_copy(signal_ref, signal_ref, local.at[1]).wait()

    def wait_image_send(k):
        def one(r, carry):
            image_copy(k, lax.rem(me + r, N)).wait_send()
            return carry

        lax.fori_loop(1, N, one, 0)

    wait_image_send(0)

    @pl.when(split)
    def _():
        wait_image_send(1)

    def image_arrival(slot):
        return pltpu.make_async_remote_copy(
            src_ref=piece_in.at[slot],
            dst_ref=piece_in.at[slot],
            send_sem=image_recv.at[slot],
            recv_sem=image_recv.at[slot],
            device_id=(plane, up_w, tick),
            device_id_type=MESH,
        )

    def hand_out(slot):
        pltpu.make_async_copy(piece_in.at[slot], image_ref.at[slot], local.at[4]).start()

    def landed(slot):
        image_arrival(slot).wait_recv()
        hand_out(slot)

    def whole_images(r, carry):
        landed(lax.rem(mine + r, 8))
        return carry

    def split_images(r, carry):
        for k in range(2):
            for h in range(2):
                landed(8 + (2 * lax.rem(plane + r, 4) + k) * 2 + h)
        return carry

    lax.fori_loop(1, 8, whole_images, 0)
    lax.fori_loop(1, 4, split_images, 0)
    for k in range(2):
        landed(8 + (2 * plane + k) * 2 + 1 - half)

    @pl.when(split)
    def _():
        landed(mine)
        for k in range(2):
            hand_out(8 + (2 * plane + k) * 2 + half)

    @pl.when(whole)
    def _():
        hand_out(mine)
        for k in range(2):
            landed(8 + (2 * plane + k) * 2 + half)

    pltpu.make_async_copy(piece_in, image_ref, local.at[4]).wait()


def finish_kernel(signal_ref, piece_ref, signal_out, image_ref, held, pieces, image, sem):
    loads, stores = [], []
    for g in range(4):
        span = pl.ds(2 * g, 2)
        loads.append(
            (
                pltpu.make_async_copy(piece_ref.at[span], pieces.at[span], sem.at[0, g]),
                pltpu.make_async_copy(
                    piece_ref.at[pl.ds(8 + 4 * g, 4)], pieces.at[pl.ds(8 + 4 * g, 4)], sem.at[1, g]
                ),
                pltpu.make_async_copy(signal_ref.at[span], held.at[span], sem.at[2, g]),
            )
        )
        low, high = pl.ds(2 * g * TB, 2 * TB), pl.ds((8 + 2 * g) * TB, 2 * TB)
        stores.append(
            (
                pltpu.make_async_copy(image.at[:, low], image_ref.at[:, low], sem.at[3, g]),
                pltpu.make_async_copy(image.at[:, high], image_ref.at[:, high], sem.at[4, g]),
                pltpu.make_async_copy(held.at[span], signal_out.at[span], sem.at[5, g]),
            )
        )
    for load in loads:
        for copy in load:
            copy.start()
    for g in range(4):
        loads[g][0].wait()
        loads[g][1].wait()
        for j in (2 * g, 2 * g + 1):
            image[:, j * TB : (j + 1) * TB] = pieces[j].astype(F32)
            image[:, (8 + j) * TB : (9 + j) * TB] = pieces[8 + 2 * j].astype(F32) + pieces[
                9 + 2 * j
            ].astype(F32)
        stores[g][0].start()
        stores[g][1].start()
        loads[g][2].wait()
        stores[g][2].start()
    for store in stores:
        for copy in store:
            copy.wait()


def finish(signal, pieces):
    return pl.pallas_call(
        finish_kernel,
        out_shape=(
            jax.ShapeDtypeStruct((8, 32, 2048), BF16),
            jax.ShapeDtypeStruct((TB, 2048), F32),
        ),
        in_specs=[ANY, ANY],
        out_specs=(ANY, ANY),
        scratch_shapes=[
            pltpu.VMEM((8, 32, 2048), BF16),
            pltpu.VMEM((24, TB, TB), BF16),
            pltpu.VMEM((TB, 2048), F32),
            pltpu.SemaphoreType.DMA((6, 4)),
        ],
        compiler_params=pltpu.CompilerParams(vmem_limit_bytes=LIMIT),
        name="finish",
    )(signal, pieces)


def fused(raw, mask, taps, blocks, owners, geo):
    dma = pltpu.SemaphoreType.DMA
    return pl.pallas_call(
        kernel,
        out_shape=(
            jax.ShapeDtypeStruct((8, 32, 2048), BF16),
            jax.ShapeDtypeStruct((24, TB, TB), BF16),
        ),
        in_specs=[HBM, VMEM, VMEM, VMEM, VMEM, HBM],
        out_specs=(ANY, ANY),
        scratch_shapes=[
            pltpu.VMEM((256, 2048), BF16),
            pltpu.VMEM((24, 2 * TB), F32),
            pltpu.VMEM((8, TB), jnp.int32),
            pltpu.VMEM((2, 256, TB), BF16),
            pltpu.VMEM((2, 16, 2048), BF16),
            pltpu.VMEM((2, 256, TB), BF16),
            pltpu.VMEM((2, 16, 2048), BF16),
            pltpu.VMEM((4, 16, TB), BF16),
            pltpu.VMEM((256, TB), F32),
            pltpu.VMEM((288 * 18, TB), F32),
            pltpu.VMEM((3, 288, 16, TB), BF16),
            pltpu.VMEM((33 * TB, 2 * TB), BF16),
            pltpu.VMEM((ROWS, TB), F32),
            pltpu.VMEM((N, 8, 32, TB), BF16),
            pltpu.VMEM((65, 32, TB), BF16),
            pltpu.VMEM((65, 32, TB), BF16),
            pltpu.VMEM((N, 8, TB), F32),
            pltpu.VMEM((2, 8, 8, TB), F32),
            pltpu.VMEM((TB, 32, TB), BF16),
            pltpu.VMEM((2, 8, 2 * TB), jnp.int32),
            pltpu.SMEM((2, 8, 2 * TB), jnp.int32),
            pltpu.VMEM((2, BLOCKS + 1, TB, TB), F32),
            pltpu.VMEM((2, N, TB, TB), BF16),
            pltpu.VMEM((24, TB, TB), BF16),
            dma((8,)),
            dma((8,)),
            dma((N,)),
            dma((2, 8)),
            dma((N,)),
            dma((2, 8)),
            dma((2, N)),
            dma((24,)),
            dma((5,)),
        ],
        compiler_params=pltpu.CompilerParams(
            vmem_limit_bytes=LIMIT, collective_id=0, has_side_effects=True
        ),
        name="fused",
    )(raw, mask, taps, blocks, owners, geo)


def shards(raw, chan_mask, kernel_rows, geometry, roi_block, roi_owner):
    signal, pieces = fused(
        raw,
        chan_mask.reshape(1, 256),
        kernel_rows[0],
        roi_block.reshape(1, -1),
        roi_owner.reshape(1, -1),
        geometry,
    )
    signal, image = finish(signal, pieces)
    return (signal.reshape(256, 2048), image)


def solution(mesh):
    in_specs = (
        P(("plane", "wire"), "tick"),
        P(("plane", "wire")),
        P("plane", None, None),
        P(),
        P(("plane", "wire", "tick")),
        P(("plane", "wire", "tick")),
    )
    out_specs = (P(("plane", "wire"), "tick"), P(("plane", "wire"), "tick"))
    return jax.shard_map(shards, mesh=mesh, in_specs=in_specs, out_specs=out_specs, check_vma=False)
```

```python
import jax
import jax.numpy as jnp
from jax import lax
from jax.experimental import pallas as pl
from jax.experimental.pallas import tpu as pltpu
from jax.sharding import PartitionSpec as P

TB = 128
N = 16
CHUNK = 64
ROWS = CHUNK * 16
EARLY = 4
BLOCKS = 22
UNROLL = BLOCKS
LIMIT = 56 << 20
MESH = pl.DeviceIdType.MESH
VMEM = pl.BlockSpec(memory_space=pltpu.VMEM)
ANY = pl.BlockSpec(memory_space=pl.ANY)
HBM = pl.BlockSpec(memory_space=pltpu.HBM)
BF16 = jnp.bfloat16
F32 = jnp.float32


def row_of(ref, index, size):
    return ref.at[pl.ds(pl.multiple_of(index, size), size)]


def build_bands(taps_ref, band_ref, first, last):
    row = lax.broadcasted_iota(jnp.int32, (TB, TB), 0)
    col = lax.broadcasted_iota(jnp.int32, (TB, TB), 1)
    upper = col >= row
    zero = jnp.zeros((TB, TB), F32)

    def pair(m, carry):
        for p in range(2):
            taps = taps_ref[pl.ds(2 * m + p, 1), :]
            low, high = [
                pltpu.roll(
                    jnp.broadcast_to(taps[:, half * TB : (half + 1) * TB], (TB, TB)),
                    0,
                    1,
                    stride=1,
                    stride_axis=0,
                )
                for half in range(2)
            ]
            pieces = (
                jnp.where(upper, zero, high),
                jnp.where(upper, high, low),
                jnp.where(upper, low, zero),
            )
            for piece in range(3):
                start = pl.multiple_of((m * 3 + piece) * TB, TB)
                band_ref[pl.ds(start, TB), p * TB : (p + 1) * TB] = pieces[piece].astype(BF16)
        return carry

    lax.fori_loop(first, last, pair, 0)


def kernel(
    raw_hbm,
    mask_ref,
    taps_ref,
    block_ref,
    owner_ref,
    geo_ref,
    signal_ref,
    image_ref,
    raw_ref,
    taps,
    roi_ref,
    edge_t,
    edge_w,
    halo_t,
    halo_w,
    halo_c,
    mask_col,
    tall,
    shifted,
    band,
    sums,
    sig,
    recv_0,
    recv_1,
    own_out,
    own_in,
    geo,
    plan_v,
    plan,
    runs,
    piece_out,
    piece_in,
    halo_send,
    halo_recv,
    own_send,
    own_recv,
    tile_send,
    tile_recv,
    image_send,
    image_recv,
    local,
):
    plane, wire, tick = lax.axis_index("plane"), lax.axis_index("wire"), lax.axis_index("tick")
    me = plane * 4 + wire
    recv = (recv_0, recv_1)
    half, inner = wire // 2, lax.rem(wire, 2)
    spot = plane * 2 + inner
    whole = jnp.logical_or(wire == 1, wire == 2)
    split = jnp.logical_not(whole)
    mine = plane * 2 + half
    up_t, down_t = lax.rem(tick + 1, 16), lax.rem(tick + 15, 16)
    up_w, down_w = lax.rem(wire + 1, 4), lax.rem(wire + 3, 4)

    def member(m):
        return (m // 4, lax.rem(m, 4), tick)

    raw_copy = pltpu.make_async_copy(raw_hbm, raw_ref, local.at[3])
    raw_copy.start()
    barrier = pltpu.get_barrier_semaphore()

    def greet(r, carry):
        pl.semaphore_signal(barrier, inc=1, device_id=member(lax.rem(me + r, N)), device_id_type=MESH)
        return carry

    has = {"t+": tick < 15, "t-": tick > 0, "w+": wire < 3, "w-": wire > 0}

    def when_all(keys, action):
        test = has[keys[0]]
        for key in keys[1:]:
            test = jnp.logical_and(test, has[key])
        pl.when(test)(action)
        return test

    for t_key, t in (("t+", up_t), ("t-", down_t)):
        for w_keys, w in (((), wire), (("w+",), up_w), (("w-",), down_w)):

            def greet_side():
                pl.semaphore_signal(barrier, inc=1, device_id=(plane, w, t), device_id_type=MESH)

            when_all((t_key, *w_keys), greet_side)
    lax.fori_loop(1, N, greet, 0)

    geo_copy = pltpu.make_async_copy(geo_ref, geo, local.at[0])
    taps[...] = jnp.zeros((24, 2 * TB), F32)
    taps[0:21, :] = taps_ref[...].astype(F32)
    roi_ref[...] = jnp.full((8, TB), -1, jnp.int32)
    roi_ref[0:1, 0:102] = block_ref[...]
    roi_ref[1:2, 0:102] = owner_ref[...]

    row = lax.broadcasted_iota(jnp.int32, (256, 256), 0)
    col = lax.broadcasted_iota(jnp.int32, (256, 256), 1)
    diag = jnp.where(row == col, mask_ref[...].astype(F32), 0.0).astype(BF16)
    mask_col[...] = jnp.dot(diag, jnp.ones((256, TB), BF16), preferred_element_type=F32)

    build_bands(taps, band, 0, EARLY)
    raw_copy.wait()
    geo_copy.start()
    for side, start in ((0, 0), (1, 15 * TB)):
        edge_t[side] = (raw_ref[:, start : start + TB].astype(F32) * mask_col[...]).astype(BF16)
    for side, start in ((0, 0), (1, 240)):
        for j in range(N):
            cols = slice(j * TB, (j + 1) * TB)
            edge_w[side, :, cols] = (
                raw_ref[start : start + 16, cols].astype(F32) * mask_col[start : start + 16, :]
            ).astype(BF16)

    ticks_near = (tick < 15).astype(jnp.int32) + (tick > 0).astype(jnp.int32)
    wires_near = 1 + (wire < 3).astype(jnp.int32) + (wire > 0).astype(jnp.int32)
    pl.semaphore_wait(barrier, 15 + ticks_near * wires_near)

    first, last = slice(0, TB), slice(15 * TB, 16 * TB)
    halo_copies = [
        pltpu.make_async_remote_copy(
            src_ref=src,
            dst_ref=dst,
            send_sem=halo_send.at[i],
            recv_sem=halo_recv.at[i],
            device_id=(plane, w, t),
            device_id_type=MESH,
        )
        for i, (src, dst, w, t) in enumerate(
            (
                (edge_t.at[1], halo_t.at[0], wire, up_t),
                (edge_t.at[0], halo_t.at[1], wire, down_t),
                (edge_w.at[1], halo_w.at[0], up_w, tick),
                (edge_w.at[0], halo_w.at[1], down_w, tick),
                (edge_w.at[1, :, last], halo_c.at[0], up_w, up_t),
                (edge_w.at[1, :, first], halo_c.at[1], up_w, down_t),
                (edge_w.at[0, :, last], halo_c.at[2], down_w, up_t),
                (edge_w.at[0, :, first], halo_c.at[3], down_w, down_t),
            )
        )
    ]
    outward = (("t+",), ("t-",), ("w+",), ("w-",), ("w+", "t+"), ("w+", "t-"), ("w-", "t+"), ("w-", "t-"))
    inward = (("t-",), ("t+",), ("w-",), ("w+",), ("w-", "t-"), ("w-", "t+"), ("w+", "t-"), ("w+", "t+"))
    landing = [halo_t.at[0], halo_t.at[1], halo_w.at[0], halo_w.at[1]] + [halo_c.at[i] for i in range(4)]
    for keys, copy in zip(outward, halo_copies):
        when_all(keys, copy.start)

    def take_halo(i):
        test = when_all(inward[i], halo_copies[i].wait_recv)

        @pl.when(jnp.logical_not(test))
        def _():
            landing[i][...] = jnp.zeros(landing[i].shape, BF16)

    def to_whole(r, turn, src, dst, send, receive):
        a = lax.rem(mine + r, 8)
        return pltpu.make_async_remote_copy(
            src_ref=src(a),
            dst_ref=dst(turn, spot),
            send_sem=send.at[a],
            recv_sem=receive.at[turn, spot],
            device_id=(a // 2, 1 + lax.rem(a, 2), tick),
            device_id_type=MESH,
        )

    def to_split(p, h, src, dst, send, receive):
        return pltpu.make_async_remote_copy(
            src_ref=src(8 + 2 * p + h),
            dst_ref=dst(h, spot),
            send_sem=send.at[8 + 2 * p + h],
            recv_sem=receive.at[h, spot],
            device_id=(p, 3 * half, tick),
            device_id_type=MESH,
        )

    def exchange(act, *refs):
        def across(i, carry):
            act(to_whole(2 * i + 1, 1, *refs))
            return carry

        def within(i, carry):
            act(to_whole(2 * i, 0, *refs))
            return carry

        def splits(r, carry):
            for h in range(2):
                act(to_split(lax.rem(plane + r, 4), h, *refs))
            return carry

        lax.fori_loop(0, 4, across, 0)
        lax.fori_loop(1, 4, within, 0)
        lax.fori_loop(1, 4, splits, 0)

        @pl.when(split)
        def _():
            act(to_whole(0, 0, *refs))

        @pl.when(whole)
        def _():
            for h in range(2):
                act(to_split(plane, h, *refs))

    def begin(copy):
        copy.start()

    def wait_send(copy):
        copy.wait_send()

    def side_of(turn):
        return jnp.where(whole, 1 - half, half) if turn else half

    def arrival(h, other, dst, receive):
        return pltpu.make_async_remote_copy(
            src_ref=dst(h, other),
            dst_ref=dst(h, other),
            send_sem=receive.at[h, other],
            recv_sem=receive.at[h, other],
            device_id=(other // 2, 2 * side_of(h) + lax.rem(other, 2), tick),
            device_id_type=MESH,
        )

    def wait_half(h, second, dst, receive):
        def one(r, carry):
            arrival(h, lax.rem(spot + r, 8), dst, receive).wait_recv()
            return carry

        lax.fori_loop(1, 8, one, 0)
        if second:

            @pl.when(whole)
            def _():
                arrival(h, spot, dst, receive).wait_recv()

    build_bands(taps, band, EARLY, 11)

    def spread(i, carry):
        wires = pl.ds(pl.multiple_of(i * 16, 16), 16)
        keep = mask_col[wires, :]
        for j in range(N):
            piece = raw_ref[wires, j * TB : (j + 1) * TB].astype(F32) * keep
            tall[pl.ds((i + 1) * 288 + j + 1, 16, stride=18), :] = piece
        return carry

    lax.fori_loop(0, 16, spread, 0)

    def window(i, carry):
        for u in range(8):
            slot = i * 8 + u
            for piece in range(3):
                shifted[piece, slot] = tall[pl.ds(slot * 18 + piece, 16), :].astype(BF16)
        return carry

    for i in (0, 1):
        take_halo(i)

    def spread_ticks(i, carry):
        wires = pl.ds(pl.multiple_of(i * 16, 16), 16)
        for side, j in ((0, 0), (1, 17)):
            tall[pl.ds((i + 1) * 288 + j, 16, stride=18), :] = halo_t[side, wires, :].astype(F32)
        return carry

    lax.fori_loop(0, 16, spread_ticks, 0)
    lax.fori_loop(CHUNK // 8, CHUNK // 8 + 4, window, 0)

    def run_chunk(base, size):
        lhs = jnp.concatenate(
            [
                shifted[piece, pl.ds(base + 6 + 2 * m, size + 1)].reshape((size + 1) * 16, TB)
                for m in range(11)
                for piece in range(3)
            ],
            axis=1,
        )
        both = jnp.dot(lhs, band[...], preferred_element_type=F32)
        sums[0 : size * 16] = both[: size * 16, :TB] + both[16:, TB:]
        tile = base // 32
        for j in range(N):
            for b in range(size // 16):
                sig[j, tile + b // 2, (b % 2) * 16 : (b % 2) * 16 + 16, :] = sums[
                    pl.ds(b * 256 + j, 16, stride=16), :
                ].astype(BF16)
        exchange(
            begin,
            lambda j: sig.at[j, pl.ds(tile, size // 32)],
            lambda h, i: recv[h].at[pl.ds(i * 8 + tile, size // 32)],
            tile_send,
            tile_recv,
        )

    own_refs = (lambda j: own_out.at[j], lambda h, i: own_in.at[h, i], own_send, own_recv)

    def share_owners():
        row = lax.broadcasted_iota(jnp.int32, (TB, TB), 0)
        hit = jnp.where(roi_ref[0:1, :] == lax.rem(row, 8) * 16 + row // 8, roi_ref[1:2, :] + 1, 0)
        table = jnp.dot(hit.astype(F32).astype(BF16), jnp.ones((TB, TB), BF16), preferred_element_type=F32)
        own_out[...] = table.reshape(N, 8, TB)

        exchange(begin, *own_refs)

        @pl.when(whole)
        def _():
            own_in[0, spot] = own_out[mine]

        @pl.when(split)
        def _():
            for h in range(2):
                own_in[h, spot] = own_out[8 + 2 * plane + h]

    def take_wires():
        for i in range(2, 8):
            take_halo(i)
        for side, base in ((0, 0), (1, 272 * 18)):
            for j in range(N):
                tall[pl.ds(base + j + 1, 16, stride=18), :] = halo_w[side, :, j * TB : (j + 1) * TB].astype(F32)
            for t, j in ((0, 0), (1, 17)):
                tall[pl.ds(base + j, 16, stride=18), :] = halo_c[side * 2 + t].astype(F32)

    chunks = 256 // CHUNK

    def step(n, carry):
        c = lax.rem(n + 1, chunks)
        pl.when(n == chunks - 2)(take_wires)
        slots = jnp.where(c == 0, 0, (c * CHUNK + 32) // 8)
        lax.fori_loop(slots, slots + CHUNK // 8, window, 0)
        run_chunk(c * CHUNK, CHUNK)
        pl.when(n == 0)(share_owners)
        return carry

    lax.fori_loop(0, chunks, step, 0)

    def store_signal(j, carry):
        pltpu.make_async_copy(
            sig.at[j], signal_ref.at[:, :, pl.ds(pl.multiple_of(j * TB, TB), TB)], local.at[1]
        ).start()
        return carry

    lax.fori_loop(0, N, store_signal, 0)

    @pl.when(whole)
    def _():
        recv[0][pl.ds(spot * 8, 8)] = sig[mine]

    @pl.when(split)
    def _():
        for h in range(2):
            recv[h][pl.ds(spot * 8, 8)] = sig[8 + 2 * plane + h]

    own_dst, tile_dst = own_refs[1], lambda h, i: recv[h].at[pl.ds(i * 8, 8)]
    wait_half(0, False, own_dst, own_recv)
    wait_half(1, True, own_dst, own_recv)

    tile = lax.broadcasted_iota(jnp.int32, (64, TB), 0)
    lane = lax.broadcasted_iota(jnp.int32, (64, TB), 1)
    place = lax.broadcasted_iota(jnp.int32, (64, 2 * TB), 1).astype(F32)
    before = (lax.broadcasted_iota(jnp.int32, (64, 64), 1) < lax.broadcasted_iota(jnp.int32, (64, 64), 0)).astype(
        F32
    )
    lower = (lax.broadcasted_iota(jnp.int32, (TB, TB), 0) < lax.broadcasted_iota(jnp.int32, (TB, TB), 1)).astype(
        F32
    )
    for h in range(2):
        side = side_of(h)
        georow = ((tile // 16) * 4 + 2 * side + lax.rem(tile // 8, 2)) * 8 + lax.rem(tile, 8)
        wanted = own_in[h].reshape(64, TB)
        member_of = jnp.where(wanted == (lane + 1).astype(F32), 1.0, 0.0)
        rank = jnp.dot(before.astype(BF16), member_of.astype(BF16), preferred_element_type=F32)
        count = jnp.sum(member_of, axis=0, keepdims=True)
        blocks = jnp.floor((count + 7.0) * 0.125)
        opening = jnp.dot(
            jnp.broadcast_to(blocks, (8, TB)).astype(BF16), lower.astype(BF16), preferred_element_type=F32
        )[0:1, :]
        found = jnp.sum(member_of, axis=1, keepdims=True)
        spot_of = jnp.sum(member_of * (opening * 8.0 + rank), axis=1, keepdims=True) - (1.0 - found)
        rank_of = jnp.sum(member_of * rank, axis=1, keepdims=True)
        here = jnp.where(spot_of == place, 1.0, 0.0)
        tile_f, geo_f = tile[:, 0:1].astype(F32), georow[:, 0:1].astype(F32)
        plan_v[h, 0:1, :] = (64.0 + jnp.sum(here * (tile_f - 64.0), axis=0, keepdims=True)).astype(jnp.int32)
        plan_v[h, 1:2, :] = jnp.sum(here * geo_f, axis=0, keepdims=True).astype(jnp.int32)
        again = jnp.where(spot_of == place * 8.0, 1.0, 0.0) * jnp.where(rank_of > 0.0, 1.0, 0.0)
        plan_v[h, 2:3, :] = jnp.sum(again, axis=0, keepdims=True).astype(jnp.int32)
        closing = jnp.where(count > 0.0, opening + blocks - 1.0, float(BLOCKS))
        plan_v[h, 3:4, 0:TB] = closing.astype(jnp.int32)
        plan_v[h, 3:4, TB : 2 * TB] = closing.astype(jnp.int32)
        plan_v[h, 4:8, :] = jnp.zeros((4, 2 * TB), jnp.int32)
        recv[h][64] = jnp.zeros((32, TB), BF16)
        runs[h, BLOCKS] = jnp.zeros((TB, TB), F32)
    plan_copy = pltpu.make_async_copy(plan_v, plan, local.at[2])
    plan_copy.start()
    geo_copy.wait()
    plan_copy.wait()

    def image_slot(p, w, h, k):
        outer = jnp.logical_or(w == 0, w == 3)
        return jnp.where(outer, 8 + (2 * p + k) * 2 + h, 2 * p + h)

    def image_copy(k, o):
        slot = image_slot(plane, wire, half, k)
        return pltpu.make_async_remote_copy(
            src_ref=piece_out.at[k, o],
            dst_ref=piece_in.at[slot],
            send_sem=image_send.at[k, o],
            recv_sem=image_recv.at[slot],
            device_id=member(o),
            device_id_type=MESH,
        )

    both_halves = jnp.where(whole, 1.0, 0.0)
    for h in range(2):
        k = 0 if h == 0 else jnp.where(whole, 0, 1)
        wait_half(h, h == 1, tile_dst, tile_recv)

        def block(b, run):
            lhs = jnp.concatenate([geo[jnp.clip(plan[h, 1, b * 8 + i], 0, TB - 1)] for i in range(8)], axis=0)
            rhs = jnp.concatenate([recv[h][jnp.clip(plan[h, 0, b * 8 + i], 0, 64)] for i in range(8)], axis=0)
            part = lax.dot_general(lhs, rhs, (((0,), (0,)), ((), ())), preferred_element_type=F32)
            run = run * plan[h, 2, b].astype(F32) + part
            runs[h, b] = run
            return run

        lax.fori_loop(0, BLOCKS, block, jnp.zeros((TB, TB), F32), unroll=UNROLL)

        for i in range(N):
            o = lax.rem(plane + 1 + i // 2, 4) * 4
            if i < 8:
                o += 2 * (1 - half) + i % 2
            else:
                o += 2 * half + lax.rem(inner + 1 + i, 2)

            def send_piece():
                now = runs[h, jnp.clip(plan[h, 3, o], 0, BLOCKS)]
                if h == 1:
                    now = now + runs[0, jnp.clip(plan[0, 3, o], 0, BLOCKS)] * both_halves
                piece_out[k, o] = now.astype(BF16)
                if i < N - 1:
                    image_copy(k, o).start()
                else:
                    piece_in[image_slot(plane, wire, half, k)] = piece_out[k, o]

            if h == 0:
                pl.when(split)(send_piece)
            else:
                send_piece()

    for keys, copy in zip(outward, halo_copies):
        when_all(keys, copy.wait_send)
    exchange(wait_send, *own_refs)
    exchange(wait_send, lambda j: sig.at[j], tile_dst, tile_send, tile_recv)
    pltpu.make_async_copy(signal_ref, signal_ref, local.at[1]).wait()

    def wait_image_send(k):
        def one(r, carry):
            image_copy(k, lax.rem(me + r, N)).wait_send()
            return carry

        lax.fori_loop(1, N, one, 0)

    wait_image_send(0)

    @pl.when(split)
    def _():
        wait_image_send(1)

    def image_arrival(slot):
        return pltpu.make_async_remote_copy(
            src_ref=piece_in.at[slot],
            dst_ref=piece_in.at[slot],
            send_sem=image_recv.at[slot],
            recv_sem=image_recv.at[slot],
            device_id=(plane, up_w, tick),
            device_id_type=MESH,
        )

    def hand_out(slot):
        pltpu.make_async_copy(piece_in.at[slot], image_ref.at[slot], local.at[4]).start()

    def landed(slot):
        image_arrival(slot).wait_recv()
        hand_out(slot)

    def whole_images(r, carry):
        landed(lax.rem(mine + r, 8))
        return carry

    def split_images(r, carry):
        for k in range(2):
            for h in range(2):
                landed(8 + (2 * lax.rem(plane + r, 4) + k) * 2 + h)
        return carry

    lax.fori_loop(1, 8, whole_images, 0)
    lax.fori_loop(1, 4, split_images, 0)
    for k in range(2):
        landed(8 + (2 * plane + k) * 2 + 1 - half)

    @pl.when(split)
    def _():
        landed(mine)
        for k in range(2):
            hand_out(8 + (2 * plane + k) * 2 + half)

    @pl.when(whole)
    def _():
        hand_out(mine)
        for k in range(2):
            landed(8 + (2 * plane + k) * 2 + half)

    pltpu.make_async_copy(piece_in, image_ref, local.at[4]).wait()


def finish_kernel(signal_ref, piece_ref, signal_out, image_ref, held, pieces, image, sem):
    loads, stores = [], []
    for g in range(4):
        span = pl.ds(2 * g, 2)
        loads.append(
            (
                pltpu.make_async_copy(piece_ref.at[span], pieces.at[span], sem.at[0, g]),
                pltpu.make_async_copy(
                    piece_ref.at[pl.ds(8 + 4 * g, 4)], pieces.at[pl.ds(8 + 4 * g, 4)], sem.at[1, g]
                ),
                pltpu.make_async_copy(signal_ref.at[span], held.at[span], sem.at[2, g]),
            )
        )
        low, high = pl.ds(2 * g * TB, 2 * TB), pl.ds((8 + 2 * g) * TB, 2 * TB)
        stores.append(
            (
                pltpu.make_async_copy(image.at[:, low], image_ref.at[:, low], sem.at[3, g]),
                pltpu.make_async_copy(image.at[:, high], image_ref.at[:, high], sem.at[4, g]),
                pltpu.make_async_copy(held.at[span], signal_out.at[span], sem.at[5, g]),
            )
        )
    for load in loads:
        for copy in load:
            copy.start()
    for g in range(4):
        loads[g][0].wait()
        loads[g][1].wait()
        for j in (2 * g, 2 * g + 1):
            image[:, j * TB : (j + 1) * TB] = pieces[j].astype(F32)
            image[:, (8 + j) * TB : (9 + j) * TB] = pieces[8 + 2 * j].astype(F32) + pieces[
                9 + 2 * j
            ].astype(F32)
        stores[g][0].start()
        stores[g][1].start()
        loads[g][2].wait()
        stores[g][2].start()
    for store in stores:
        for copy in store:
            copy.wait()


def finish(signal, pieces):
    return pl.pallas_call(
        finish_kernel,
        out_shape=(
            jax.ShapeDtypeStruct((8, 32, 2048), BF16),
            jax.ShapeDtypeStruct((TB, 2048), F32),
        ),
        in_specs=[ANY, ANY],
        out_specs=(ANY, ANY),
        scratch_shapes=[
            pltpu.VMEM((8, 32, 2048), BF16),
            pltpu.VMEM((24, TB, TB), BF16),
            pltpu.VMEM((TB, 2048), F32),
            pltpu.SemaphoreType.DMA((6, 4)),
        ],
        compiler_params=pltpu.CompilerParams(vmem_limit_bytes=LIMIT),
        name="finish",
    )(signal, pieces)


def fused(raw, mask, taps, blocks, owners, geo):
    dma = pltpu.SemaphoreType.DMA
    return pl.pallas_call(
        kernel,
        out_shape=(
            jax.ShapeDtypeStruct((8, 32, 2048), BF16),
            jax.ShapeDtypeStruct((24, TB, TB), BF16),
        ),
        in_specs=[HBM, VMEM, VMEM, VMEM, VMEM, HBM],
        out_specs=(ANY, ANY),
        scratch_shapes=[
            pltpu.VMEM((256, 2048), BF16),
            pltpu.VMEM((24, 2 * TB), F32),
            pltpu.VMEM((8, TB), jnp.int32),
            pltpu.VMEM((2, 256, TB), BF16),
            pltpu.VMEM((2, 16, 2048), BF16),
            pltpu.VMEM((2, 256, TB), BF16),
            pltpu.VMEM((2, 16, 2048), BF16),
            pltpu.VMEM((4, 16, TB), BF16),
            pltpu.VMEM((256, TB), F32),
            pltpu.VMEM((290 * 18 + 12, TB), F32),
            pltpu.VMEM((3, 288, 16, TB), BF16),
            pltpu.VMEM((33 * TB, 2 * TB), BF16),
            pltpu.VMEM((ROWS + 32, TB), F32),
            pltpu.VMEM((N, 8, 32, TB), BF16),
            pltpu.VMEM((65, 32, TB), BF16),
            pltpu.VMEM((65, 32, TB), BF16),
            pltpu.VMEM((N, 8, TB), F32),
            pltpu.VMEM((2, 8, 8, TB), F32),
            pltpu.VMEM((TB, 32, TB), BF16),
            pltpu.VMEM((2, 8, 2 * TB), jnp.int32),
            pltpu.SMEM((2, 8, 2 * TB), jnp.int32),
            pltpu.VMEM((2, BLOCKS + 1, TB, TB), F32),
            pltpu.VMEM((2, N, TB, TB), BF16),
            pltpu.VMEM((24, TB, TB), BF16),
            dma((8,)),
            dma((8,)),
            dma((N,)),
            dma((2, 8)),
            dma((N,)),
            dma((2, 8)),
            dma((2, N)),
            dma((24,)),
            dma((5,)),
        ],
        compiler_params=pltpu.CompilerParams(
            vmem_limit_bytes=LIMIT, collective_id=0, has_side_effects=True
        ),
        name="fused",
    )(raw, mask, taps, blocks, owners, geo)


def shards(raw, chan_mask, kernel_rows, geometry, roi_block, roi_owner):
    signal, pieces = fused(
        raw,
        chan_mask.reshape(1, 256),
        kernel_rows[0],
        roi_block.reshape(1, -1),
        roi_owner.reshape(1, -1),
        geometry,
    )
    signal, image = finish(signal, pieces)
    return (signal.reshape(256, 2048), image)


def solution(mesh):
    in_specs = (
        P(("plane", "wire"), "tick"),
        P(("plane", "wire")),
        P("plane", None, None),
        P(),
        P(("plane", "wire", "tick")),
        P(("plane", "wire", "tick")),
    )
    out_specs = (P(("plane", "wire"), "tick"), P(("plane", "wire"), "tick"))
    return jax.shard_map(shards, mesh=mesh, in_specs=in_specs, out_specs=out_specs, check_vma=False)
```

```python
import jax
import jax.numpy as jnp
from jax import lax
from jax.experimental import pallas as pl
from jax.experimental.pallas import tpu as pltpu
from jax.sharding import PartitionSpec as P

TB = 128
N = 16
CHUNK = 64
ROWS = CHUNK * 16
BLOCKS = 22
UNROLL = BLOCKS
LIMIT = 56 << 20
MESH = pl.DeviceIdType.MESH
VMEM = pl.BlockSpec(memory_space=pltpu.VMEM)
ANY = pl.BlockSpec(memory_space=pl.ANY)
HBM = pl.BlockSpec(memory_space=pltpu.HBM)
BF16 = jnp.bfloat16
F32 = jnp.float32


def row_of(ref, index, size):
    return ref.at[pl.ds(pl.multiple_of(index, size), size)]


def build_bands(taps_ref, band_ref):
    row = lax.broadcasted_iota(jnp.int32, (TB, TB), 0)
    col = lax.broadcasted_iota(jnp.int32, (TB, TB), 1)
    upper = col >= row
    zero = jnp.zeros((TB, TB), F32)

    def pair(m, carry):
        for p in range(2):
            taps = taps_ref[pl.ds(2 * m + p, 1), :]
            low, high = [
                pltpu.roll(
                    jnp.broadcast_to(taps[:, half * TB : (half + 1) * TB], (TB, TB)),
                    0,
                    1,
                    stride=1,
                    stride_axis=0,
                )
                for half in range(2)
            ]
            pieces = (
                jnp.where(upper, zero, high),
                jnp.where(upper, high, low),
                jnp.where(upper, low, zero),
            )
            for piece in range(3):
                start = pl.multiple_of((m * 3 + piece) * TB, TB)
                band_ref[pl.ds(start, TB), p * TB : (p + 1) * TB] = pieces[piece].astype(BF16)
        return carry

    lax.fori_loop(0, 11, pair, 0)


def kernel(
    raw_hbm,
    mask_ref,
    taps_ref,
    block_ref,
    owner_ref,
    geo_ref,
    signal_ref,
    image_ref,
    raw_ref,
    taps,
    roi_ref,
    edge_t,
    edge_w,
    halo_t,
    halo_w,
    halo_c,
    mask_col,
    tall,
    shifted,
    band,
    sums,
    sig,
    recv_0,
    recv_1,
    own_out,
    own_in,
    geo,
    plan_v,
    plan,
    runs,
    piece_out,
    piece_in,
    halo_send,
    halo_recv,
    own_send,
    own_recv,
    tile_send,
    tile_recv,
    image_send,
    image_recv,
    local,
):
    plane, wire, tick = lax.axis_index("plane"), lax.axis_index("wire"), lax.axis_index("tick")
    me = plane * 4 + wire
    recv = (recv_0, recv_1)
    half, inner = wire // 2, lax.rem(wire, 2)
    spot = plane * 2 + inner
    whole = jnp.logical_or(wire == 1, wire == 2)
    split = jnp.logical_not(whole)
    mine = plane * 2 + half
    up_t, down_t = lax.rem(tick + 1, 16), lax.rem(tick + 15, 16)
    up_w, down_w = lax.rem(wire + 1, 4), lax.rem(wire + 3, 4)

    def member(m):
        return (m // 4, lax.rem(m, 4), tick)

    barrier = pltpu.get_barrier_semaphore()

    def greet(r, carry):
        pl.semaphore_signal(barrier, inc=1, device_id=member(lax.rem(me + r, N)), device_id_type=MESH)
        return carry

    has = {"t+": tick < 15, "t-": tick > 0, "w+": wire < 3, "w-": wire > 0}

    def when_all(keys, action):
        test = has[keys[0]]
        for key in keys[1:]:
            test = jnp.logical_and(test, has[key])
        pl.when(test)(action)
        return test

    for t_key, t in (("t+", up_t), ("t-", down_t)):
        for w_keys, w in (((), wire), (("w+",), up_w), (("w-",), down_w)):

            def greet_side():
                pl.semaphore_signal(barrier, inc=1, device_id=(plane, w, t), device_id_type=MESH)

            when_all((t_key, *w_keys), greet_side)
    lax.fori_loop(1, N, greet, 0)

    raw_copy = pltpu.make_async_copy(raw_hbm, raw_ref, local.at[3])
    raw_copy.start()
    geo_copy = pltpu.make_async_copy(geo_ref, geo, local.at[0])
    taps[...] = jnp.zeros((24, 2 * TB), F32)
    taps[0:21, :] = taps_ref[...].astype(F32)
    roi_ref[...] = jnp.full((8, TB), -1, jnp.int32)
    roi_ref[0:1, 0:102] = block_ref[...]
    roi_ref[1:2, 0:102] = owner_ref[...]

    row = lax.broadcasted_iota(jnp.int32, (256, 256), 0)
    col = lax.broadcasted_iota(jnp.int32, (256, 256), 1)
    diag = jnp.where(row == col, mask_ref[...].astype(F32), 0.0).astype(BF16)
    mask_col[...] = jnp.dot(diag, jnp.ones((256, TB), BF16), preferred_element_type=F32)

    raw_copy.wait()
    geo_copy.start()
    for side, start in ((0, 0), (1, 15 * TB)):
        edge_t[side] = (raw_ref[:, start : start + TB].astype(F32) * mask_col[...]).astype(BF16)
    for side, start in ((0, 0), (1, 240)):
        for j in range(N):
            cols = slice(j * TB, (j + 1) * TB)
            edge_w[side, :, cols] = (
                raw_ref[start : start + 16, cols].astype(F32) * mask_col[start : start + 16, :]
            ).astype(BF16)

    ticks_near = (tick < 15).astype(jnp.int32) + (tick > 0).astype(jnp.int32)
    wires_near = 1 + (wire < 3).astype(jnp.int32) + (wire > 0).astype(jnp.int32)
    pl.semaphore_wait(barrier, 15 + ticks_near * wires_near)

    first, last = slice(0, TB), slice(15 * TB, 16 * TB)
    halo_copies = [
        pltpu.make_async_remote_copy(
            src_ref=src,
            dst_ref=dst,
            send_sem=halo_send.at[i],
            recv_sem=halo_recv.at[i],
            device_id=(plane, w, t),
            device_id_type=MESH,
        )
        for i, (src, dst, w, t) in enumerate(
            (
                (edge_t.at[1], halo_t.at[0], wire, up_t),
                (edge_t.at[0], halo_t.at[1], wire, down_t),
                (edge_w.at[1], halo_w.at[0], up_w, tick),
                (edge_w.at[0], halo_w.at[1], down_w, tick),
                (edge_w.at[1, :, last], halo_c.at[0], up_w, up_t),
                (edge_w.at[1, :, first], halo_c.at[1], up_w, down_t),
                (edge_w.at[0, :, last], halo_c.at[2], down_w, up_t),
                (edge_w.at[0, :, first], halo_c.at[3], down_w, down_t),
            )
        )
    ]
    outward = (("t+",), ("t-",), ("w+",), ("w-",), ("w+", "t+"), ("w+", "t-"), ("w-", "t+"), ("w-", "t-"))
    inward = (("t-",), ("t+",), ("w-",), ("w+",), ("w-", "t-"), ("w-", "t+"), ("w+", "t-"), ("w+", "t+"))
    landing = [halo_t.at[0], halo_t.at[1], halo_w.at[0], halo_w.at[1]] + [halo_c.at[i] for i in range(4)]
    for keys, copy in zip(outward, halo_copies):
        when_all(keys, copy.start)

    def take_halo(i):
        test = when_all(inward[i], halo_copies[i].wait_recv)

        @pl.when(jnp.logical_not(test))
        def _():
            landing[i][...] = jnp.zeros(landing[i].shape, BF16)

    def to_whole(r, turn, src, dst, send, receive):
        a = lax.rem(mine + r, 8)
        return pltpu.make_async_remote_copy(
            src_ref=src(a),
            dst_ref=dst(turn, spot),
            send_sem=send.at[a],
            recv_sem=receive.at[turn, spot],
            device_id=(a // 2, 1 + lax.rem(a, 2), tick),
            device_id_type=MESH,
        )

    def to_split(p, h, src, dst, send, receive):
        return pltpu.make_async_remote_copy(
            src_ref=src(8 + 2 * p + h),
            dst_ref=dst(h, spot),
            send_sem=send.at[8 + 2 * p + h],
            recv_sem=receive.at[h, spot],
            device_id=(p, 3 * half, tick),
            device_id_type=MESH,
        )

    def exchange(act, *refs):
        def across(i, carry):
            act(to_whole(2 * i + 1, 1, *refs))
            return carry

        def within(i, carry):
            act(to_whole(2 * i, 0, *refs))
            return carry

        def splits(r, carry):
            for h in range(2):
                act(to_split(lax.rem(plane + r, 4), h, *refs))
            return carry

        lax.fori_loop(0, 4, across, 0)
        lax.fori_loop(1, 4, within, 0)
        lax.fori_loop(1, 4, splits, 0)

        @pl.when(split)
        def _():
            act(to_whole(0, 0, *refs))

        @pl.when(whole)
        def _():
            for h in range(2):
                act(to_split(plane, h, *refs))

    def begin(copy):
        copy.start()

    def wait_send(copy):
        copy.wait_send()

    def side_of(turn):
        return jnp.where(whole, 1 - half, half) if turn else half

    def arrival(h, other, dst, receive):
        return pltpu.make_async_remote_copy(
            src_ref=dst(h, other),
            dst_ref=dst(h, other),
            send_sem=receive.at[h, other],
            recv_sem=receive.at[h, other],
            device_id=(other // 2, 2 * side_of(h) + lax.rem(other, 2), tick),
            device_id_type=MESH,
        )

    def wait_half(h, second, dst, receive):
        def one(r, carry):
            arrival(h, lax.rem(spot + r, 8), dst, receive).wait_recv()
            return carry

        lax.fori_loop(1, 8, one, 0)
        if second:

            @pl.when(whole)
            def _():
                arrival(h, spot, dst, receive).wait_recv()

    build_bands(taps, band)

    def spread(i, carry):
        wires = pl.ds(pl.multiple_of(i * 16, 16), 16)
        keep = mask_col[wires, :]
        for j in range(N):
            piece = raw_ref[wires, j * TB : (j + 1) * TB].astype(F32) * keep
            tall[pl.ds((i + 1) * 288 + j + 1, 16, stride=18), :] = piece
        return carry

    lax.fori_loop(0, 16, spread, 0)

    def window(i, carry):
        for u in range(8):
            slot = i * 8 + u
            for piece in range(3):
                shifted[piece, slot] = tall[pl.ds(slot * 18 + piece, 16), :].astype(BF16)
        return carry

    for i in (0, 1):
        take_halo(i)

    def spread_ticks(i, carry):
        wires = pl.ds(pl.multiple_of(i * 16, 16), 16)
        for side, j in ((0, 0), (1, 17)):
            tall[pl.ds((i + 1) * 288 + j, 16, stride=18), :] = halo_t[side, wires, :].astype(F32)
        return carry

    lax.fori_loop(0, 16, spread_ticks, 0)
    lax.fori_loop(CHUNK // 8, CHUNK // 8 + 4, window, 0)

    def run_chunk(base, size):
        lhs = jnp.concatenate(
            [
                shifted[piece, pl.ds(base + 6 + 2 * m, size + 1)].reshape((size + 1) * 16, TB)
                for m in range(11)
                for piece in range(3)
            ],
            axis=1,
        )
        both = jnp.dot(lhs, band[...], preferred_element_type=F32)
        sums[0 : size * 16] = both[: size * 16, :TB] + both[16:, TB:]
        tile = base // 32
        for j in range(N):
            for b in range(size // 16):
                sig[j, tile + b // 2, (b % 2) * 16 : (b % 2) * 16 + 16, :] = sums[
                    pl.ds(b * 256 + j, 16, stride=16), :
                ].astype(BF16)
        exchange(
            begin,
            lambda j: sig.at[j, pl.ds(tile, size // 32)],
            lambda h, i: recv[h].at[pl.ds(i * 8 + tile, size // 32)],
            tile_send,
            tile_recv,
        )

    own_refs = (lambda j: own_out.at[j], lambda h, i: own_in.at[h, i], own_send, own_recv)

    def share_owners():
        row = lax.broadcasted_iota(jnp.int32, (TB, TB), 0)
        hit = jnp.where(roi_ref[0:1, :] == lax.rem(row, 8) * 16 + row // 8, roi_ref[1:2, :] + 1, 0)
        table = jnp.dot(hit.astype(F32).astype(BF16), jnp.ones((TB, TB), BF16), preferred_element_type=F32)
        own_out[...] = table.reshape(N, 8, TB)

        exchange(begin, *own_refs)

        @pl.when(whole)
        def _():
            own_in[0, spot] = own_out[mine]

        @pl.when(split)
        def _():
            for h in range(2):
                own_in[h, spot] = own_out[8 + 2 * plane + h]

    def take_wires():
        for i in range(2, 8):
            take_halo(i)
        for side, base in ((0, 0), (1, 272 * 18)):
            for j in range(N):
                tall[pl.ds(base + j + 1, 16, stride=18), :] = halo_w[side, :, j * TB : (j + 1) * TB].astype(F32)
            for t, j in ((0, 0), (1, 17)):
                tall[pl.ds(base + j, 16, stride=18), :] = halo_c[side * 2 + t].astype(F32)

    chunks = 256 // CHUNK

    def step(n, carry):
        c = lax.rem(n + 1, chunks)
        pl.when(n == chunks - 2)(take_wires)
        slots = jnp.where(c == 0, 0, (c * CHUNK + 32) // 8)
        lax.fori_loop(slots, slots + CHUNK // 8, window, 0)
        run_chunk(c * CHUNK, CHUNK)
        pl.when(n == 0)(share_owners)
        return carry

    lax.fori_loop(0, chunks, step, 0)

    def store_signal(j, carry):
        pltpu.make_async_copy(
            sig.at[j], signal_ref.at[:, :, pl.ds(pl.multiple_of(j * TB, TB), TB)], local.at[1]
        ).start()
        return carry

    lax.fori_loop(0, N, store_signal, 0)

    @pl.when(whole)
    def _():
        recv[0][pl.ds(spot * 8, 8)] = sig[mine]

    @pl.when(split)
    def _():
        for h in range(2):
            recv[h][pl.ds(spot * 8, 8)] = sig[8 + 2 * plane + h]

    own_dst, tile_dst = own_refs[1], lambda h, i: recv[h].at[pl.ds(i * 8, 8)]
    wait_half(0, False, own_dst, own_recv)
    wait_half(1, True, own_dst, own_recv)

    tile = lax.broadcasted_iota(jnp.int32, (64, TB), 0)
    lane = lax.broadcasted_iota(jnp.int32, (64, TB), 1)
    place = lax.broadcasted_iota(jnp.int32, (64, 2 * TB), 1).astype(F32)
    before = (lax.broadcasted_iota(jnp.int32, (64, 64), 1) < lax.broadcasted_iota(jnp.int32, (64, 64), 0)).astype(
        F32
    )
    lower = (lax.broadcasted_iota(jnp.int32, (TB, TB), 0) < lax.broadcasted_iota(jnp.int32, (TB, TB), 1)).astype(
        F32
    )
    for h in range(2):
        side = side_of(h)
        georow = ((tile // 16) * 4 + 2 * side + lax.rem(tile // 8, 2)) * 8 + lax.rem(tile, 8)
        wanted = own_in[h].reshape(64, TB)
        member_of = jnp.where(wanted == (lane + 1).astype(F32), 1.0, 0.0)
        rank = jnp.dot(before.astype(BF16), member_of.astype(BF16), preferred_element_type=F32)
        count = jnp.sum(member_of, axis=0, keepdims=True)
        blocks = jnp.floor((count + 7.0) * 0.125)
        opening = jnp.dot(
            jnp.broadcast_to(blocks, (8, TB)).astype(BF16), lower.astype(BF16), preferred_element_type=F32
        )[0:1, :]
        found = jnp.sum(member_of, axis=1, keepdims=True)
        spot_of = jnp.sum(member_of * (opening * 8.0 + rank), axis=1, keepdims=True) - (1.0 - found)
        rank_of = jnp.sum(member_of * rank, axis=1, keepdims=True)
        here = jnp.where(spot_of == place, 1.0, 0.0)
        tile_f, geo_f = tile[:, 0:1].astype(F32), georow[:, 0:1].astype(F32)
        plan_v[h, 0:1, :] = (64.0 + jnp.sum(here * (tile_f - 64.0), axis=0, keepdims=True)).astype(jnp.int32)
        plan_v[h, 1:2, :] = jnp.sum(here * geo_f, axis=0, keepdims=True).astype(jnp.int32)
        again = jnp.where(spot_of == place * 8.0, 1.0, 0.0) * jnp.where(rank_of > 0.0, 1.0, 0.0)
        plan_v[h, 2:3, :] = jnp.sum(again, axis=0, keepdims=True).astype(jnp.int32)
        closing = jnp.where(count > 0.0, opening + blocks - 1.0, float(BLOCKS))
        plan_v[h, 3:4, 0:TB] = closing.astype(jnp.int32)
        plan_v[h, 3:4, TB : 2 * TB] = closing.astype(jnp.int32)
        plan_v[h, 4:8, :] = jnp.zeros((4, 2 * TB), jnp.int32)
        recv[h][64] = jnp.zeros((32, TB), BF16)
        runs[h, BLOCKS] = jnp.zeros((TB, TB), F32)
    plan_copy = pltpu.make_async_copy(plan_v, plan, local.at[2])
    plan_copy.start()
    geo_copy.wait()
    plan_copy.wait()

    def image_slot(p, w, h, k):
        outer = jnp.logical_or(w == 0, w == 3)
        return jnp.where(outer, 8 + (2 * p + k) * 2 + h, 2 * p + h)

    def image_copy(k, o):
        slot = image_slot(plane, wire, half, k)
        return pltpu.make_async_remote_copy(
            src_ref=piece_out.at[k, o],
            dst_ref=piece_in.at[slot],
            send_sem=image_send.at[k, o],
            recv_sem=image_recv.at[slot],
            device_id=member(o),
            device_id_type=MESH,
        )

    both_halves = jnp.where(whole, 1.0, 0.0)
    for h in range(2):
        k = 0 if h == 0 else jnp.where(whole, 0, 1)
        wait_half(h, h == 1, tile_dst, tile_recv)

        def block(b, run):
            lhs = jnp.concatenate([geo[jnp.clip(plan[h, 1, b * 8 + i], 0, TB - 1)] for i in range(8)], axis=0)
            rhs = jnp.concatenate([recv[h][jnp.clip(plan[h, 0, b * 8 + i], 0, 64)] for i in range(8)], axis=0)
            part = lax.dot_general(lhs, rhs, (((0,), (0,)), ((), ())), preferred_element_type=F32)
            run = run * plan[h, 2, b].astype(F32) + part
            runs[h, b] = run
            return run

        lax.fori_loop(0, BLOCKS, block, jnp.zeros((TB, TB), F32), unroll=UNROLL)

        for i in range(N):
            o = lax.rem(plane + 1 + i // 2, 4) * 4
            if i < 8:
                o += 2 * (1 - half) + i % 2
            else:
                o += 2 * half + lax.rem(inner + 1 + i, 2)

            def send_piece():
                now = runs[h, jnp.clip(plan[h, 3, o], 0, BLOCKS)]
                if h == 1:
                    now = now + runs[0, jnp.clip(plan[0, 3, o], 0, BLOCKS)] * both_halves
                piece_out[k, o] = now.astype(BF16)
                if i < N - 1:
                    image_copy(k, o).start()
                else:
                    piece_in[image_slot(plane, wire, half, k)] = piece_out[k, o]

            if h == 0:
                pl.when(split)(send_piece)
            else:
                send_piece()

    for keys, copy in zip(outward, halo_copies):
        when_all(keys, copy.wait_send)
    exchange(wait_send, *own_refs)
    exchange(wait_send, lambda j: sig.at[j], tile_dst, tile_send, tile_recv)
    pltpu.make_async_copy(signal_ref, signal_ref, local.at[1]).wait()

    def wait_image_send(k):
        def one(r, carry):
            image_copy(k, lax.rem(me + r, N)).wait_send()
            return carry

        lax.fori_loop(1, N, one, 0)

    wait_image_send(0)

    @pl.when(split)
    def _():
        wait_image_send(1)

    def image_arrival(slot):
        return pltpu.make_async_remote_copy(
            src_ref=piece_in.at[slot],
            dst_ref=piece_in.at[slot],
            send_sem=image_recv.at[slot],
            recv_sem=image_recv.at[slot],
            device_id=(plane, up_w, tick),
            device_id_type=MESH,
        )

    def hand_out(slot):
        pltpu.make_async_copy(piece_in.at[slot], image_ref.at[slot], local.at[4]).start()

    def landed(slot):
        image_arrival(slot).wait_recv()
        hand_out(slot)

    def whole_images(r, carry):
        landed(lax.rem(mine + r, 8))
        return carry

    def split_images(r, carry):
        for k in range(2):
            for h in range(2):
                landed(8 + (2 * lax.rem(plane + r, 4) + k) * 2 + h)
        return carry

    lax.fori_loop(1, 8, whole_images, 0)
    lax.fori_loop(1, 4, split_images, 0)
    for k in range(2):
        landed(8 + (2 * plane + k) * 2 + 1 - half)

    @pl.when(split)
    def _():
        landed(mine)
        for k in range(2):
            hand_out(8 + (2 * plane + k) * 2 + half)

    @pl.when(whole)
    def _():
        hand_out(mine)
        for k in range(2):
            landed(8 + (2 * plane + k) * 2 + half)

    pltpu.make_async_copy(piece_in, image_ref, local.at[4]).wait()


def finish_kernel(signal_ref, piece_ref, signal_out, image_ref, held, pieces, image, sem):
    loads, stores = [], []
    for g in range(4):
        span = pl.ds(2 * g, 2)
        loads.append(
            (
                pltpu.make_async_copy(piece_ref.at[span], pieces.at[span], sem.at[0, g]),
                pltpu.make_async_copy(
                    piece_ref.at[pl.ds(8 + 4 * g, 4)], pieces.at[pl.ds(8 + 4 * g, 4)], sem.at[1, g]
                ),
                pltpu.make_async_copy(signal_ref.at[span], held.at[span], sem.at[2, g]),
            )
        )
        low, high = pl.ds(2 * g * TB, 2 * TB), pl.ds((8 + 2 * g) * TB, 2 * TB)
        stores.append(
            (
                pltpu.make_async_copy(image.at[:, low], image_ref.at[:, low], sem.at[3, g]),
                pltpu.make_async_copy(image.at[:, high], image_ref.at[:, high], sem.at[4, g]),
                pltpu.make_async_copy(held.at[span], signal_out.at[span], sem.at[5, g]),
            )
        )
    for i in (2, 0, 1):
        for load in loads:
            load[i].start()
    for g in range(4):
        loads[g][2].wait()
        stores[g][2].start()
    for g in range(4):
        loads[g][0].wait()
        loads[g][1].wait()
        for j in (2 * g, 2 * g + 1):
            image[:, j * TB : (j + 1) * TB] = pieces[j].astype(F32)
            image[:, (8 + j) * TB : (9 + j) * TB] = pieces[8 + 2 * j].astype(F32) + pieces[
                9 + 2 * j
            ].astype(F32)
        stores[g][0].start()
        stores[g][1].start()
    for store in stores:
        for copy in store:
            copy.wait()


def finish(signal, pieces):
    return pl.pallas_call(
        finish_kernel,
        out_shape=(
            jax.ShapeDtypeStruct((8, 32, 2048), BF16),
            jax.ShapeDtypeStruct((TB, 2048), F32),
        ),
        in_specs=[ANY, ANY],
        out_specs=(ANY, ANY),
        scratch_shapes=[
            pltpu.VMEM((8, 32, 2048), BF16),
            pltpu.VMEM((24, TB, TB), BF16),
            pltpu.VMEM((TB, 2048), F32),
            pltpu.SemaphoreType.DMA((6, 4)),
        ],
        compiler_params=pltpu.CompilerParams(vmem_limit_bytes=LIMIT),
        name="finish",
    )(signal, pieces)


def fused(raw, mask, taps, blocks, owners, geo):
    dma = pltpu.SemaphoreType.DMA
    return pl.pallas_call(
        kernel,
        out_shape=(
            jax.ShapeDtypeStruct((8, 32, 2048), BF16),
            jax.ShapeDtypeStruct((24, TB, TB), BF16),
        ),
        in_specs=[HBM, VMEM, VMEM, VMEM, VMEM, HBM],
        out_specs=(ANY, ANY),
        scratch_shapes=[
            pltpu.VMEM((256, 2048), BF16),
            pltpu.VMEM((24, 2 * TB), F32),
            pltpu.VMEM((8, TB), jnp.int32),
            pltpu.VMEM((2, 256, TB), BF16),
            pltpu.VMEM((2, 16, 2048), BF16),
            pltpu.VMEM((2, 256, TB), BF16),
            pltpu.VMEM((2, 16, 2048), BF16),
            pltpu.VMEM((4, 16, TB), BF16),
            pltpu.VMEM((256, TB), F32),
            pltpu.VMEM((290 * 18 + 12, TB), F32),
            pltpu.VMEM((3, 288, 16, TB), BF16),
            pltpu.VMEM((33 * TB, 2 * TB), BF16),
            pltpu.VMEM((ROWS + 32, TB), F32),
            pltpu.VMEM((N, 8, 32, TB), BF16),
            pltpu.VMEM((65, 32, TB), BF16),
            pltpu.VMEM((65, 32, TB), BF16),
            pltpu.VMEM((N, 8, TB), F32),
            pltpu.VMEM((2, 8, 8, TB), F32),
            pltpu.VMEM((TB, 32, TB), BF16),
            pltpu.VMEM((2, 8, 2 * TB), jnp.int32),
            pltpu.SMEM((2, 8, 2 * TB), jnp.int32),
            pltpu.VMEM((2, BLOCKS + 1, TB, TB), F32),
            pltpu.VMEM((2, N, TB, TB), BF16),
            pltpu.VMEM((24, TB, TB), BF16),
            dma((8,)),
            dma((8,)),
            dma((N,)),
            dma((2, 8)),
            dma((N,)),
            dma((2, 8)),
            dma((2, N)),
            dma((24,)),
            dma((5,)),
        ],
        compiler_params=pltpu.CompilerParams(
            vmem_limit_bytes=LIMIT, collective_id=0, has_side_effects=True
        ),
        name="fused",
    )(raw, mask, taps, blocks, owners, geo)


def shards(raw, chan_mask, kernel_rows, geometry, roi_block, roi_owner):
    signal, pieces = fused(
        raw,
        chan_mask.reshape(1, 256),
        kernel_rows[0],
        roi_block.reshape(1, -1),
        roi_owner.reshape(1, -1),
        geometry,
    )
    signal, image = finish(signal, pieces)
    return (signal.reshape(256, 2048), image)


def solution(mesh):
    in_specs = (
        P(("plane", "wire"), "tick"),
        P(("plane", "wire")),
        P("plane", None, None),
        P(),
        P(("plane", "wire", "tick")),
        P(("plane", "wire", "tick")),
    )
    out_specs = (P(("plane", "wire"), "tick"), P(("plane", "wire"), "tick"))
    return jax.shard_map(shards, mesh=mesh, in_specs=in_specs, out_specs=out_specs, check_vma=False)
```
